32 devices in a mesh: section: 4 (over y, x), slab: 8 (over z, core).
Axes of the slice: x: 2, y: 2, z: 4, core: 2. Of those that a mesh axis runs over, the one named last changes fastest.
Arguments:
- features_in: bfloat16 [2, 256, 8, 2, 64], P(None, None, 'slab'), may hold values from -6 to 6
- labels: int32 [2, 8, 2, 64], P(None, 'slab'), may hold values from 0 to 5
- offsets: int32 [3, 3], replicated, may hold values from -1 to 1, as said below
- conv_weight: bfloat16 [4, 3, 3, 3, 256, 256], P('section'), may hold values from -0.078125 to 0.078125
- branch_weight: bfloat16 [4, 256, 256], P('section'), may hold values from -0.375 to 0.375
- head_weight: bfloat16 [256, 3], replicated, may hold values from -0.375 to 0.375
Outputs:
- loss: float32 [], replicated
- grad_conv: float32 [4, 3, 3, 3, 256, 256], P('section')
- grad_branch: float32 [4, 256, 256], P('section')
- grad_head: float32 [256, 3], replicated
The draws below stay inside these ranges and needn't reach their ends.
Inputs may be any that keep to these rules, and one draw needn't show every extreme that they name: Row j of the offsets has a nonzero entry j.
All inputs are finite; a program needn't handle non-finite values.
Results may differ from the reference program's by a relative error of at most 0.0023.
Values may be sent and summed in bfloat16 or wider, within the bound.
No kernel may reach another device: no remote copies, remote signals or barrier semaphores. Data moves between devices by JAX's collectives and lax.ppermute only.
A program may use at most 64 MiB of HBM per device.

```python
import jax
import jax.numpy as jnp
from jax import lax

C = 256
OFFS = 3
MICRO = 2
ROWS = 2
COLS = 64
SECTIONS = 4
DEPTH = 8


def draw_labels(key, part):
    coarse = jax.random.randint(key, (MICRO, DEPTH, ROWS // 2 + 1, COLS // 4 + 1), 0, 6)
    coarse = coarse.at[0, 0, 0, 0].set(5)
    coarse = coarse.at[0, 0, 0, 1].set(0)
    expanded = jnp.repeat(jnp.repeat(coarse, 2, axis=2), 4, axis=3)
    return expanded[:, :DEPTH, :ROWS, :COLS].astype(jnp.int32)


def draw_offsets(key, part):
    first_key, second_key = jax.random.split(key)
    extra = jax.random.randint(first_key, (OFFS, 3), -1, 2)
    flip_sign = 2 * jax.random.randint(second_key, (), 0, 2) - 1
    diagonal_values = jnp.array([-1, 1, 0], dtype=jnp.int32) + flip_sign * jnp.array([0, 0, 1], dtype=jnp.int32)
    identity = jnp.eye(OFFS, 3, dtype=jnp.int32)
    return jnp.where(identity > 0, diagonal_values[:, None], extra).astype(jnp.int32)


def levels(stream_key, extent, shards, smallest, largest):
    loudness, own = 1.0, jax.random.fold_in(stream_key, 6)
    for dim, blocks in shards:
        steps = jnp.exp(jax.random.uniform(jax.random.fold_in(own, dim), (blocks,), jnp.float32, smallest / len(shards), largest / len(shards)))
        loudness = loudness * jnp.repeat(steps, extent[dim] // blocks).reshape([-1 if axis == dim else 1 for axis in range(len(extent))])
    return loudness


def bell_draw(rng, dims, spread, limit, shards=(), kind=jnp.bfloat16):
    values = spread * jax.random.normal(rng, dims, jnp.float32)
    if shards:
        values = values * levels(rng, dims, shards, -0.22, 0.18)
    return jnp.clip(values, -limit, limit).astype(kind)


def setup_inputs(seed: int = 0) -> dict:
    streams_of = jax.random.split(jax.random.key(seed), 7)
    return {
        "features_in": bell_draw(streams_of[0], (MICRO, C, DEPTH, ROWS, COLS), 1.0, 6.0, ((2, 8),)),
        "labels": draw_labels(jax.random.fold_in(streams_of[6], 71), 0),
        "offsets": draw_offsets(jax.random.fold_in(streams_of[6], 71), 0),
        "conv_weight": bell_draw(streams_of[3], (SECTIONS, 3, 3, 3, C, C), (27 * C) ** -0.5, 0.078125, ((0, 4),)),
        "branch_weight": bell_draw(streams_of[4], (SECTIONS, C, C), C ** -0.5, 0.375, ((0, 4),)),
        "head_weight": bell_draw(streams_of[5], (C, OFFS), C ** -0.5, 0.375),
    }


loss_scale = 1024.0


def shifted_windows(padded, depth, height, width):
    windows = []
    for first in range(3):
        for second in range(3):
            for third in range(3):
                windows.append(padded[:, first:first + depth, second:second + height, third:third + width])
    return windows


def conv_full(source, kernel):
    depth, height, width = source.shape[1], source.shape[2], source.shape[3]
    padded = jnp.pad(source.astype(jnp.float32), ((0, 0), (1, 1), (1, 1), (1, 1)))
    flat_kernel = kernel.astype(jnp.float32).reshape(27, kernel.shape[3], kernel.shape[4])
    result = jnp.zeros((kernel.shape[4], depth, height, width), jnp.float32)
    for offset_id, window in enumerate(shifted_windows(padded, depth, height, width)):
        result = result + jnp.einsum('izyx,io->ozyx', window, flat_kernel[offset_id])
    return result


def conv_transposed_full(cotangent, kernel):
    flipped = jnp.swapaxes(jnp.flip(kernel, (0, 1, 2)), 3, 4)
    return conv_full(cotangent, flipped)


def weight_grad_full(source, cotangent):
    depth, height, width = source.shape[1], source.shape[2], source.shape[3]
    padded = jnp.pad(source.astype(jnp.float32), ((0, 0), (1, 1), (1, 1), (1, 1)))
    cot_float = cotangent.astype(jnp.float32)
    pieces = [jnp.einsum('izyx,ozyx->io', window, cot_float) for window in shifted_windows(padded, depth, height, width)]
    return jnp.stack(pieces).reshape(3, 3, 3, source.shape[0], cotangent.shape[0])


def silu_slope(preact):
    logistic = jax.nn.sigmoid(preact)
    return logistic * (1.0 + preact * (1.0 - logistic))


def affinity_targets(volume, offsets):
    padded = jnp.pad(volume, 1)
    target_maps = []
    for channel in range(OFFS):
        start = (1 + offsets[channel]).astype(jnp.int32)
        neighbor = lax.dynamic_slice(padded, (start[0], start[1], start[2]), volume.shape)
        same = (neighbor == volume) & (volume != 0)
        target_maps.append(jnp.where(same, 1.0, 0.0).astype(jnp.float32))
    return jnp.stack(target_maps)


def reference(features_in, labels, offsets, conv_weight, branch_weight, head_weight):
    half = SECTIONS // 2
    count = MICRO * OFFS * DEPTH * ROWS * COLS
    grad_conv = jnp.zeros(conv_weight.shape, jnp.float32)
    grad_branch = jnp.zeros(branch_weight.shape, jnp.float32)
    grad_head = jnp.zeros(head_weight.shape, jnp.float32)
    loss_total = jnp.zeros((), jnp.float32)
    head_float = head_weight.astype(jnp.float32)
    for micro_id in range(MICRO):
        current = features_in[micro_id]
        inputs, branches, preacts, outputs = [], [], [], []
        for section_id in range(SECTIONS):
            branch = current if section_id < half else outputs[SECTIONS - 1 - section_id]
            preact = conv_full(current, conv_weight[section_id]) + jnp.einsum(
                'io,izyx->ozyx', branch_weight[section_id].astype(jnp.float32), branch.astype(jnp.float32))
            output = jax.nn.silu(preact).astype(jnp.bfloat16)
            inputs.append(current)
            branches.append(branch)
            preacts.append(preact)
            outputs.append(output)
            current = output
        logits = jnp.einsum('co,czyx->ozyx', head_float, current.astype(jnp.float32))
        targets = affinity_targets(labels[micro_id], offsets)
        loss_total = loss_total + jnp.sum(jax.nn.softplus(logits) - targets * logits)
        logit_grad = (loss_scale * (jax.nn.sigmoid(logits) - targets) / count).astype(jnp.bfloat16)
        grad_head = grad_head + jnp.einsum('czyx,ozyx->co', current.astype(jnp.float32), logit_grad.astype(jnp.float32))
        head_cotangent = jnp.einsum('co,ozyx->czyx', head_float, logit_grad.astype(jnp.float32))
        skip_grads = {}
        passed = None
        for section_id in reversed(range(SECTIONS)):
            if section_id == SECTIONS - 1:
                upstream = head_cotangent
            else:
                upstream = passed.astype(jnp.float32)
            if section_id < half:
                upstream = upstream + skip_grads[section_id].astype(jnp.float32)
            pre_grad = (upstream * silu_slope(preacts[section_id])).astype(jnp.bfloat16)
            grad_conv = grad_conv.at[section_id].add(weight_grad_full(inputs[section_id], pre_grad))
            grad_branch = grad_branch.at[section_id].add(jnp.einsum(
                'izyx,ozyx->io', branches[section_id].astype(jnp.float32), pre_grad.astype(jnp.float32)))
            branch_grad = jnp.einsum('io,ozyx->izyx', branch_weight[section_id].astype(jnp.float32), pre_grad.astype(jnp.float32))
            input_grad = conv_transposed_full(pre_grad, conv_weight[section_id])
            if section_id < half:
                passed = (input_grad + branch_grad).astype(jnp.bfloat16)
            else:
                passed = input_grad.astype(jnp.bfloat16)
                skip_grads[SECTIONS - 1 - section_id] = branch_grad.astype(jnp.bfloat16)
    return loss_total / count, grad_conv, grad_branch, grad_head
```

```python
import functools

import jax
import jax.numpy as jnp
from jax import lax
from jax.experimental import pallas as pl
from jax.experimental.pallas import tpu as pltpu
from jax.sharding import PartitionSpec as P

loss_scale = 1024.0
BF = jnp.bfloat16
F32 = jnp.float32
PAD = 8
VMEM_LIMIT = 56 * 1024 * 1024


class Dims:
    def __init__(self, sections, slabs, micro, channels, depth, rows, cols, offs):
        self.sections, self.half = sections, sections // 2
        self.slabs, self.micro = slabs, micro
        self.C, self.D, self.R, self.W, self.offs = channels, depth, rows, cols, offs
        self.G = depth * rows
        self.parts = slabs // micro
        self.own = cols // self.parts
        self.count = micro * offs * depth * rows * cols

    def fwd(self, t):
        return 2 * (self.sections - 1) - t

    def rows_of(self, k):
        return (self.own + 2 * k) * self.G


def group_mask(dm, kz, ky):
    g = lax.broadcasted_iota(jnp.int32, (1, dm.G, dm.C), 1)
    d = g // dm.R + kz
    r = g % dm.R + ky
    return (d >= 0) & (d < dm.D) & (r >= 0) & (r < dm.R)


def column_mask(dm, base, k, width):
    col = lax.broadcasted_iota(jnp.int32, (width, dm.G, dm.C), 0) + (base - k)
    return (col >= 0) & (col < dm.W)


def spread(dm, xf, x27, width, sign):
    G, C = dm.G, dm.C
    rin = (width + 2) * G
    for kz in range(3):
        for ky in range(3):
            dz, dy = sign * (kz - 1), sign * (ky - 1)
            delta = dz * dm.R + dy
            part = xf[PAD + delta:PAD + delta + rin, :]
            if kz != 1 or ky != 1:
                part = part.reshape(width + 2, G, C)
                part = jnp.where(group_mask(dm, dz, dy), part, 0.0).reshape(rin, C)
            part = part.astype(BF)
            for kx in range(3):
                first = (1 + sign * (kx - 1)) * G
                tap = (kz * 3 + ky) * 3 + kx
                x27[0:width * G, tap * C:(tap + 1) * C] = part[first:first + width * G]


def dot(a, b):
    return lax.dot_general(a, b, (((1,), (0,)), ((), ())), preferred_element_type=F32)


def dot_nt(a, b):
    return lax.dot_general(a, b, (((1,), (1,)), ((), ())), preferred_element_type=F32)


def dot_tn(a, b):
    return lax.dot_general(a, b, (((0,), (0,)), ((), ())), preferred_element_type=F32)


def stage(dm, xf, x, rin):
    xf[PAD:PAD + rin, :] = x.astype(F32)


def preact(dm, t, xf, x27, x_ref, skip_ref, w_ref, b_ref):
    k = dm.fwd(t)
    width = dm.own + 2 * k
    ro, rin = width * dm.G, (width + 2) * dm.G
    stage(dm, xf, x_ref[0:rin, :], rin)
    spread(dm, xf, x27, width, 1)
    branch = x_ref[dm.G:dm.G + ro, :] if t <= dm.half else skip_ref[0:ro, :]
    return dot(x27[0:ro, :], w_ref[...]) + dot(branch, b_ref[...])


def silu_masked(dm, base, k, pre):
    width = dm.own + 2 * k
    value = pre * (1.0 / (1.0 + jnp.exp(-pre)))
    value = value.reshape(width, dm.G, dm.C)
    value = jnp.where(column_mask(dm, base, k, width), value, 0.0)
    return value.reshape(width * dm.G, dm.C).astype(BF)


def pre_gradient(dm, base, k, upstream, pre):
    width = dm.own + 2 * k
    sig = 1.0 / (1.0 + jnp.exp(-pre))
    value = upstream * (sig * (1.0 + pre * (1.0 - sig)))
    value = value.reshape(width, dm.G, dm.C)
    value = jnp.where(column_mask(dm, base, k, width), value, 0.0)
    return value.reshape(width * dm.G, dm.C).astype(BF)


def forward_kernel(dm, t, has_skip_in, has_mirror, *refs):
    refs = list(refs)
    base_ref, x_ref, w_ref, b_ref = refs[:4]
    at = 4
    skip_ref = None
    if has_skip_in:
        skip_ref = refs[at]
        at += 1
    y_ref, pre_ref = refs[at], refs[at + 1]
    at += 2
    if has_mirror:
        mirror_ref = refs[at]
        at += 1
    xf, x27 = refs[at], refs[at + 1]
    base = base_ref[0]
    k = dm.fwd(t)
    pre = preact(dm, t, xf, x27, x_ref, skip_ref, w_ref, b_ref)
    y = silu_masked(dm, base, k, pre)
    y_ref[...] = y
    first = (k - t) * dm.G
    pre_ref[...] = pre[first:first + dm.rows_of(t)]
    if has_mirror:
        keep = dm.fwd(dm.sections - 1 - t)
        first = (k - keep) * dm.G
        mirror_ref[...] = y[first:first + dm.rows_of(keep)]


def back_conv(dm, t, pg, xf, x27, wt_ref, b_ref, msg_ref):
    width = dm.own + 2 * (t - 1)
    stage(dm, xf, pg, dm.rows_of(t))
    spread(dm, xf, x27, width, -1)
    grad = dot(x27[0:width * dm.G, :], wt_ref[...])
    if t <= dm.half:
        grad = grad + dot_nt(pg[dm.G:dm.G + width * dm.G], b_ref[...])
    msg_ref[0:width * dm.G, :] = grad.astype(BF)


def last_kernel(dm, *refs):
    (base_ref, x_ref, w_ref, b_ref, skip_ref, wt_ref, head_ref, head_t_ref, target_ref) = refs[:9]
    msg_ref, pgx_ref, skip_out, xf, x27 = refs[9:]
    t = dm.sections - 1
    base = base_ref[0]
    G, C, own = dm.G, dm.C, dm.own
    ro, mid = dm.rows_of(t), t * G
    pre = preact(dm, t, xf, x27, x_ref, skip_ref, w_ref, b_ref)
    y = silu_masked(dm, base, t, pre)
    logits = dot(y, head_ref[...])
    target = target_ref[...]
    lane = lax.broadcasted_iota(jnp.int32, logits.shape, 1)
    sig = 1.0 / (1.0 + jnp.exp(-logits))
    lg = (loss_scale * (sig - target) / dm.count)
    lg = jnp.where(lane < dm.offs, lg, 0.0).astype(BF)
    own_logits = logits[mid:mid + own * G]
    term = jnp.maximum(own_logits, 0.0) + jnp.log(1.0 + jnp.exp(-jnp.abs(own_logits)))
    term = term - target[mid:mid + own * G] * own_logits
    term = jnp.where(lane[0:own * G] < dm.offs, term, 0.0)
    loss = jnp.sum(jnp.sum(term, axis=0, keepdims=True), axis=1, keepdims=True)
    head_part = dot_tn(lg[mid:mid + own * G], y[mid:mid + own * G])
    row = lax.broadcasted_iota(jnp.int32, (8, C), 0)
    carry = jnp.where(row < dm.offs, head_part[0:8], jnp.where(row == dm.offs, loss, 0.0))
    pieces = []
    for _ in range(3):
        piece = carry.astype(BF).astype(F32)
        pieces.append(piece)
        carry = carry - piece
    carry = jnp.concatenate(pieces + [jnp.zeros((8, C), F32)], axis=0).astype(BF)
    upstream = dot(lg, head_t_ref[...])
    pg = pre_gradient(dm, base, t, upstream, pre)
    pgx_ref[0:own * G, :] = pg[mid:mid + own * G]
    pgx_ref[own * G:own * G + 32, :] = carry
    back_conv(dm, t, pg, xf, x27, wt_ref, b_ref, msg_ref)
    end = dm.rows_of(t - 1)
    msg_ref[end:end + 32, :] = carry
    if t > dm.half:
        m = dm.sections - 1 - t
        first = (t - m) * G
        skip_out[...] = dot_nt(pg[first:first + dm.rows_of(m)], b_ref[...]).astype(BF)


def backward_kernel(dm, t, has_skip_in, *refs):
    refs = list(refs)
    base_ref, down_ref, pre_ref = refs[:3]
    at = 3
    if t > 0:
        wt_ref, b_ref = refs[at:at + 2]
        at += 2
    if has_skip_in:
        skip_ref = refs[at]
        at += 1
    pgx_ref = refs[at]
    at += 1
    if t > 0:
        msg_ref = refs[at]
        at += 1
        if t > dm.half:
            skip_out = refs[at]
            at += 1
        xf, x27 = refs[at:at + 2]
    base = base_ref[0]
    ro = dm.rows_of(t)
    upstream = down_ref[0:ro, :].astype(F32)
    if has_skip_in:
        upstream = upstream + skip_ref[0:ro, :].astype(F32)
    pg = pre_gradient(dm, base, t, upstream, pre_ref[...])
    mid, size = t * dm.G, dm.own * dm.G
    carry = down_ref[ro:ro + 32, :]
    pgx_ref[0:size, :] = pg[mid:mid + size]
    pgx_ref[size:size + 32, :] = carry
    if t > 0:
        back_conv(dm, t, pg, xf, x27, wt_ref, b_ref, msg_ref)
        end = dm.rows_of(t - 1)
        msg_ref[end:end + 32, :] = carry
        if t > dm.half:
            m = dm.sections - 1 - t
            first = (t - m) * dm.G
            skip_out[...] = dot_nt(pg[first:first + dm.rows_of(m)], b_ref[...]).astype(BF)


def turn_kernel(dm, *refs):
    q_ref = refs[0]
    blocks = refs[1:1 + dm.slabs]
    xt_ref, bt_ref = refs[1 + dm.slabs:]
    size = dm.own * dm.G
    for e in range(dm.micro):
        for r in range(dm.parts):
            block = blocks[e * dm.parts + r]
            place = lax.rem(q_ref[0] + (dm.parts - r), dm.parts) + e * dm.parts
            at = pl.multiple_of(place * size, size)
            xt_ref[:, pl.ds(at, size)] = jnp.transpose(block[0:size, :])
            bt_ref[:, pl.ds(at, size)] = jnp.transpose(block[size:2 * size, :])


def weight_kernel(dm, *refs):
    q_ref, xt_ref, bt_ref = refs[:3]
    blocks = refs[3:3 + dm.slabs]
    grad_ref, mix_ref, head_ref, loss_ref, full, part, sums = refs[3 + dm.slabs:]
    G, C, W = dm.G, dm.C, dm.W
    size = dm.own * G
    span = (W + 2) * G
    rows = dm.micro * span
    step = pl.program_id(0)

    @pl.when(step == 0)
    def _():
        total = jnp.zeros((8, C), F32)
        for e in range(dm.micro):
            start = PAD + e * span
            full[start:start + G, :] = jnp.zeros((G, C), F32)
            full[start + (W + 1) * G:start + span, :] = jnp.zeros((G, C), F32)
            for r in range(dm.parts):
                block = blocks[e * dm.parts + r]
                place = lax.rem(q_ref[0] + (dm.parts - r), dm.parts)
                at = pl.multiple_of(start + G + place * size, 8)
                full[pl.ds(at, size), :] = block[0:size, :].astype(F32)
                carry = block[size:size + 32, :].astype(F32)
                slot = lax.rem(q_ref[1] + (dm.micro - e), dm.micro) * dm.parts + place
                sums[slot] = (carry[0:8] + carry[8:16]) + carry[16:24]
        for slot in range(dm.slabs):
            total = total + sums[slot]
        head_ref[...] = total
        loss_ref[...] = total[dm.offs:dm.offs + 1, 0:1] / dm.count

    kz = step // 3 - 1
    ky = step % 3 - 1
    shift = kz * dm.R + ky
    value = pltpu.roll(full[PAD:PAD + rows, :], lax.rem(shift + rows, rows), 0)
    value = value.reshape(dm.micro * (W + 2), G, C)
    value = jnp.where(group_mask(dm, -kz, -ky), value, 0.0)
    part[...] = value.reshape(rows, C).astype(BF)
    xt = xt_ref[...]
    for kx in range(3):
        total = None
        for e in range(dm.micro):
            first = e * span + (2 - kx) * G
            one = dot(xt[:, e * W * G:(e + 1) * W * G], part[first:first + W * G, :])
            total = one if total is None else total + one
        grad_ref[kx] = total

    @pl.when(step == 4)
    def _():
        total = None
        for e in range(dm.micro):
            first = e * span + G
            one = dot(bt_ref[:, e * W * G:(e + 1) * W * G], part[first:first + W * G, :])
            total = one if total is None else total + one
        mix_ref[...] = total


def whole():
    return pl.BlockSpec(memory_space=pltpu.VMEM)


def scalar():
    return pl.BlockSpec(memory_space=pltpu.SMEM)


def shape(rows, cols, kind):
    return jax.ShapeDtypeStruct((rows, cols), kind)


def call(name, kernel, base, operands, outs, scratch, flops):
    moved = sum(a.size * a.dtype.itemsize for a in operands)
    moved += sum(o.shape[0] * o.shape[1] * jnp.dtype(o.dtype).itemsize for o in outs)
    return pl.pallas_call(
        kernel,
        name=name,
        out_shape=outs,
        in_specs=[scalar()] + [whole()] * len(operands),
        out_specs=[whole()] * len(outs),
        scratch_shapes=scratch,
        compiler_params=pltpu.CompilerParams(vmem_limit_bytes=VMEM_LIMIT),
        cost_estimate=pl.CostEstimate(flops=flops, bytes_accessed=moved, transcendentals=0),
    )(base, *operands)


def conv_scratch(dm, rin, ro):
    return [
        pltpu.VMEM((rin + 2 * PAD, dm.C), F32),
        pltpu.VMEM((ro, 27 * dm.C), BF),
    ]


def body(features_in, labels, offsets, conv_weight, branch_weight, head_weight):
    n = lax.axis_size("section")
    slabs = lax.axis_size("slab")
    micro, C, thick, R, W = features_in.shape
    dm = Dims(n, slabs, micro, C, thick * slabs, R, W, offsets.shape[0])
    G, D, own, parts, half = dm.G, dm.D, dm.own, dm.parts, dm.half
    section = lax.axis_index("section")
    slab = lax.axis_index("slab")
    c, q = slab % micro, slab // micro
    base = jnp.reshape(q * own, (1,)).astype(jnp.int32)
    q_arr = jnp.stack([q, c]).astype(jnp.int32)
    size = own * G

    def hop(x, source, target):
        return lax.ppermute(x, "section", [(source, target)])

    def rotate(x, r):
        pairs = [(p * micro + e, ((p + r) % parts) * micro + e) for p in range(parts) for e in range(micro)]
        return lax.ppermute(x, "slab", pairs)

    def swap(x, e):
        pairs = [(p * micro + i, p * micro + (i + e) % micro) for p in range(parts) for i in range(micro)]
        return lax.ppermute(x, "slab", pairs)

    def gather(block):
        found = [[block] + [rotate(block, r) for r in range(1, parts)]]
        for e in range(1, micro):
            found.append([swap(b, e) for b in found[0]])
        return sum(found, [])

    kernel = conv_weight[0].reshape(27 * C, C)
    kernel_t = jnp.swapaxes(conv_weight[0].reshape(27, C, C), 1, 2).reshape(27 * C, C)
    mixing = branch_weight[0]

    wing = dm.fwd(0) + 1
    wide = own + 2 * wing
    cells = jnp.transpose(features_in, (0, 4, 2, 3, 1)).reshape(micro, W, thick * R, C)
    marks = labels.astype(BF).reshape(micro, 1, thick * R, W)
    marks = jnp.pad(marks, ((0, 0), (0, 0), (0, 0), (0, C - W)))
    cells = jnp.concatenate([cells, marks], axis=1)
    pieces = {0: lax.dynamic_index_in_dim(cells, c, 0, keepdims=False)}
    for e in range(1, micro):
        pieces[e] = swap(lax.dynamic_index_in_dim(cells, (c + e) % micro, 0, keepdims=False), e)

    def by_place(found, me, count):
        placed = []
        for p in range(count):
            value = found[0]
            for r in range(1, count):
                value = jnp.where((me + (count - r)) % count == p, found[r], value)
            placed.append(value)
        return placed

    chip = jnp.concatenate(by_place(pieces, c, micro), axis=1)
    padded = jnp.pad(chip[:W], ((wing, wing), (0, 0), (0, 0)))

    def window(place):
        view = lax.dynamic_slice_in_dim(padded, place * own, wide, 0)
        return jnp.concatenate([view, chip[W:]], axis=0)

    found = {0: window(q)}
    for r in range(1, parts):
        found[r] = rotate(window((q + r) % parts), r)
    first = jnp.concatenate(by_place(found, q, parts), axis=1)
    current = first[:wide].reshape(wide * G, C)
    crop = first[wide, :, :W].reshape(D, R, W)

    crop_pad = jnp.pad(crop, 1)
    maps = []
    for channel in range(dm.offs):
        at = 1 + offsets[channel]
        neighbor = lax.dynamic_slice(crop_pad, (at[0], at[1], at[2]), crop.shape)
        maps.append(jnp.where((neighbor == crop) & (crop != 0), 1.0, 0.0).astype(F32))
    targets = jnp.stack(maps, axis=-1)
    targets = jnp.pad(targets, ((0, 0), (0, 0), (n - 1, n - 1), (0, 128 - dm.offs)))
    targets = lax.dynamic_slice_in_dim(targets, q * own, own + 2 * (n - 1), 2)
    targets = jnp.transpose(targets, (2, 0, 1, 3)).reshape(dm.rows_of(n - 1), 128)
    head = jnp.pad(head_weight, ((0, 0), (0, 128 - dm.offs)))
    head_t = jnp.transpose(head)

    own_x, own_b, pres, mirrors = [], [], [], {}
    for t in range(n - 1):
        k = dm.fwd(t)
        begin = (k + 1) * G
        own_x.append(current[begin:begin + size])
        has_skip, has_mirror = t > half, t < half - 1
        operands = [current, kernel, mixing]
        if has_skip:
            skip = mirrors[t]
            operands.append(skip)
            own_b.append(skip[k * G:k * G + size])
        else:
            own_b.append(own_x[-1])
        outs = [shape(dm.rows_of(k), C, BF), shape(dm.rows_of(t), C, F32)]
        if has_mirror:
            outs.append(shape(dm.rows_of(dm.fwd(n - 1 - t)), C, BF))
        results = call(
            f"forward_{t}",
            functools.partial(forward_kernel, dm, t, has_skip, has_mirror),
            base, operands, outs,
            conv_scratch(dm, dm.rows_of(k + 1), dm.rows_of(k)),
            2 * dm.rows_of(k) * 28 * C * C,
        )
        pres.append(results[1])
        current = hop(results[0], t, t + 1)
        if has_mirror:
            later, current = lax.optimization_barrier((results[2], current))
            mirrors[n - 1 - t] = hop(later, t, n - 1 - t)

    t = n - 1
    own_x.append(current[(t + 1) * G:(t + 1) * G + size])
    skip = mirrors.get(t, current[G:G + dm.rows_of(t)])
    own_b.append(skip[t * G:t * G + size])
    outs = [
        shape(dm.rows_of(t - 1) + 32, C, BF),
        shape(size + 32, C, BF),
        shape(dm.rows_of(0), C, BF),
    ]
    results = call(
        "forward_last",
        functools.partial(last_kernel, dm),
        base,
        [current, kernel, mixing, skip, kernel_t, head, head_t, targets],
        outs,
        conv_scratch(dm, dm.rows_of(t + 1), dm.rows_of(t)),
        4 * dm.rows_of(t) * 28 * C * C,
    )
    own_pg = {t: results[1]}
    skip_grads = {0: hop(results[2], t, 0)}
    down = hop(results[0], t, t - 1)

    def mine(values):
        value = values[0]
        for s in range(1, n):
            value = jnp.where(section == s, values[s], value)
        return value

    held = jnp.concatenate([mine(own_x), mine(own_b)], axis=0)
    held, down = lax.optimization_barrier((held, down))
    held = gather(held)
    cells_all = micro * W * G
    xt, bt = call(
        "turn",
        functools.partial(turn_kernel, dm),
        q_arr, held,
        [shape(C, cells_all, BF), shape(C, cells_all, BF)],
        [], 1000,
    )

    for t in range(n - 2, -1, -1):
        has_skip = t < half - 1
        operands = [down, pres[t]]
        if t > 0:
            operands += [kernel_t, mixing]
        if has_skip:
            operands.append(skip_grads[t])
        outs = [shape(size + 32, C, BF)]
        scratch = []
        if t > 0:
            outs.append(shape(dm.rows_of(t - 1) + 32, C, BF))
            if t > half:
                outs.append(shape(dm.rows_of(n - 1 - t), C, BF))
            scratch = conv_scratch(dm, dm.rows_of(t), dm.rows_of(t - 1))
        results = call(
            f"backward_{t}",
            functools.partial(backward_kernel, dm, t, has_skip),
            base, operands, outs, scratch,
            2 * dm.rows_of(max(t - 1, 0)) * 28 * C * C if t > 0 else 1000,
        )
        own_pg[t] = results[0]
        if t > 0:
            down = hop(results[1], t, t - 1)
            if t > half:
                skip_grads[n - 1 - t] = hop(results[2], t, n - 1 - t)

    blocks = gather(mine(own_pg))
    span = (W + 2) * G
    grad, mix, heads, loss = pl.pallas_call(
        functools.partial(weight_kernel, dm),
        name="weights",
        grid=(9,),
        out_shape=[
            jax.ShapeDtypeStruct((27, C, C), F32),
            shape(C, C, F32),
            shape(8, C, F32),
            shape(1, 1, F32),
        ],
        in_specs=[scalar()] + [whole()] * (2 + slabs),
        out_specs=[pl.BlockSpec((3, C, C), lambda i: (i, 0, 0)), whole(), whole(), whole()],
        scratch_shapes=[
            pltpu.VMEM((micro * span + 2 * PAD, C), F32),
            pltpu.VMEM((micro * span, C), BF),
            pltpu.VMEM((slabs, 8, C), F32),
        ],
        compiler_params=pltpu.CompilerParams(vmem_limit_bytes=VMEM_LIMIT),
        cost_estimate=pl.CostEstimate(
            flops=2 * cells_all * 28 * C * C, bytes_accessed=28 * C * C * 4, transcendentals=0
        ),
    )(q_arr, xt, bt, *blocks)
    grad_head = jnp.transpose(heads[:dm.offs])
    return (
        loss[0, 0],
        grad.reshape((1, 3, 3, 3, C, C)),
        mix[None],
        grad_head,
    )


def solution(mesh):
    placed = (
        P(None, None, "slab", None, None),
        P(None, "slab", None, None),
        P(),
        P("section", None, None, None, None, None),
        P("section", None, None),
        P(),
    )
    return jax.shard_map(
        body,
        mesh=mesh,
        in_specs=placed,
        out_specs=(P(), P("section", None, None, None, None, None), P("section", None, None), P()),
        check_vma=False,
    )
```

```python
import functools
import math

import jax
import jax.numpy as jnp
from jax import lax
from jax.experimental import pallas as pl
from jax.experimental.pallas import tpu as pltpu
from jax.sharding import PartitionSpec as P


loss_scale = 1024.0
BF = jnp.bfloat16
F32 = jnp.float32
PAD = 8
SPARE = 6 * 1024 * 1024


class Dims:
    def __init__(self, sections, slabs, micro, channels, depth, rows, cols, offs):
        self.sections, self.half = sections, sections // 2
        self.slabs, self.micro = slabs, micro
        self.C, self.D, self.R, self.W, self.offs = channels, depth, rows, cols, offs
        self.G = depth * rows
        self.parts = slabs // micro
        self.own = cols // self.parts
        self.count = micro * offs * depth * rows * cols

    def fwd(self, t):
        return 2 * (self.sections - 1) - t

    def rows_of(self, k):
        return (self.own + 2 * k) * self.G


def group_mask(dm, kz, ky):
    g = lax.broadcasted_iota(jnp.int32, (1, dm.G, dm.C), 1)
    d = g // dm.R + kz
    r = g % dm.R + ky
    return (d >= 0) & (d < dm.D) & (r >= 0) & (r < dm.R)


def column_mask(dm, base, k, width):
    col = lax.broadcasted_iota(jnp.int32, (width, dm.G, dm.C), 0) + (base - k)
    return (col >= 0) & (col < dm.W)


def spread(dm, xf, x27, width, sign):
    G, C = dm.G, dm.C
    rin = (width + 2) * G
    for kz in range(3):
        for ky in range(3):
            dz, dy = sign * (kz - 1), sign * (ky - 1)
            delta = dz * dm.R + dy
            part = xf[PAD + delta:PAD + delta + rin, :]
            if kz != 1 or ky != 1:
                part = part.reshape(width + 2, G, C)
                part = jnp.where(group_mask(dm, dz, dy), part, 0.0).reshape(rin, C)
            part = part.astype(BF)
            for kx in range(3):
                first = (1 + sign * (kx - 1)) * G
                tap = (kz * 3 + ky) * 3 + kx
                x27[0:width * G, tap * C:(tap + 1) * C] = part[first:first + width * G]


def dot(a, b):
    return lax.dot_general(a, b, (((1,), (0,)), ((), ())), preferred_element_type=F32)


def dot_nt(a, b):
    return lax.dot_general(a, b, (((1,), (1,)), ((), ())), preferred_element_type=F32)


def dot_tn(a, b):
    return lax.dot_general(a, b, (((0,), (0,)), ((), ())), preferred_element_type=F32)


def stage(xf, x, rin):
    xf[PAD:PAD + rin, :] = x.astype(F32)


def preact(dm, t, xf, x27, skip_ref, w_ref, b_ref):
    width = dm.own + 2 * dm.fwd(t)
    ro = width * dm.G
    spread(dm, xf, x27, width, 1)
    if t <= dm.half:
        branch = x27[0:ro, 13 * dm.C:14 * dm.C]
    else:
        branch = skip_ref[0:ro, :]
    return dot(x27[0:ro, :], w_ref[...]) + dot(branch, b_ref[...])


def silu_masked(dm, base, k, pre):
    width = dm.own + 2 * k
    value = pre * (1.0 / (1.0 + jnp.exp(-pre)))
    value = value.reshape(width, dm.G, dm.C)
    value = jnp.where(column_mask(dm, base, k, width), value, 0.0)
    return value.reshape(width * dm.G, dm.C).astype(BF)


def pre_gradient(dm, base, k, upstream, pre):
    width = dm.own + 2 * k
    sig = 1.0 / (1.0 + jnp.exp(-pre))
    value = upstream * (sig * (1.0 + pre * (1.0 - sig)))
    value = value.reshape(width, dm.G, dm.C)
    value = jnp.where(column_mask(dm, base, k, width), value, 0.0)
    return value.reshape(width * dm.G, dm.C).astype(BF)


def forward_kernel(dm, t, has_skip_in, has_mirror, *refs):
    refs = list(refs)
    me_ref, x_ref, w_ref, b_ref = refs[:4]
    at = 4
    skip_ref = kept_ref = None
    if has_skip_in:
        skip_ref = refs[at]
        at += 1
    if t > 0:
        kept_ref = refs[at]
        at += 1
    y_ref, pre_ref, own_ref = refs[at:at + 3]
    at += 3
    if has_mirror:
        mirror_ref = refs[at]
        at += 1
    if t == 0:
        lab_ref = refs[at]
        at += 1
        wide = dm.own + 2 * (dm.fwd(0) + 1)
        lab_ref[...] = x_ref[...].astype(F32)[:, wide, :]
    xf, x27 = refs[at:at + 2]

    @pl.when(me_ref[2] == t)
    def _():
        base = me_ref[0] * dm.own
        k = dm.fwd(t)
        if t == 0:
            gather_cells(dm, x_ref, xf)
        else:
            stage(xf, x_ref[...], dm.rows_of(k + 1))
        size, mid = dm.own * dm.G, (k + 1) * dm.G
        own_ref[...] = xf[PAD + mid:PAD + mid + size, :].astype(BF)
        pre = preact(dm, t, xf, x27, skip_ref, w_ref, b_ref)
        first = (k - t) * dm.G
        pre_ref[...] = pre[first:first + dm.rows_of(t)]
        y = silu_masked(dm, base, k, pre)
        y_ref[...] = y
        if has_mirror:
            keep = dm.fwd(dm.sections - 1 - t)
            first = (k - keep) * dm.G
            mirror_ref[...] = y[first:first + dm.rows_of(keep)]

    if t > 0:
        @pl.when(me_ref[2] != t)
        def _():
            own_ref[...] = kept_ref[...]


def pack_kernel(dm, wing, cols, me_ref, f_ref, l_ref, out_ref, xs, marks):
    C, W, own = dm.C, dm.W, dm.own
    layers = f_ref.shape[0] // dm.micro
    front = -(-wing // 8) * 8
    marks[...] = jnp.zeros(marks.shape, F32)
    marks[0:dm.micro * layers, 0:W] = l_ref[...].astype(F32)
    xs[0:front, :] = jnp.zeros((front, C), F32)
    xs[front + W:, :] = jnp.zeros((xs.shape[0] - front - W, C), F32)
    row = lax.broadcasted_iota(jnp.int32, (cols, C), 0)
    for e in range(dm.micro):
        for layer in range(layers):
            at = e * layers + layer
            xs[front:front + W, :] = f_ref[at].astype(F32)
            mark = marks[at:at + 1, :]
            for p in range(dm.parts):
                start = front + p * own - wing
                value = jnp.where(row == own + 2 * wing, mark, xs[start:start + cols, :])
                first = ((p * dm.micro + e) * layers + layer) * cols
                out_ref[first:first + cols, :] = value.astype(BF)


def gather_cells(dm, x_ref, xf):
    rows = (dm.own + 2 * (dm.fwd(0) + 1)) * dm.G
    cells = jnp.transpose(x_ref[...].astype(F32), (1, 0, 2))
    cells = cells.reshape(cells.shape[0] * dm.G, dm.C)
    xf[PAD:PAD + rows, :] = cells[0:rows]


def load_kernel(chunks, w_ref, b_ref, out_ref, out_b_ref, sems):
    rows = w_ref.shape[0] // chunks
    copies = []
    for i in range(chunks):
        part = pl.ds(i * rows, rows)
        copies.append(pltpu.make_async_copy(w_ref.at[part], out_ref.at[part], sems.at[i]))
        copies[i].start()
    copies.append(pltpu.make_async_copy(b_ref, out_b_ref, sems.at[chunks]))
    copies[chunks].start()
    for copy in copies:
        copy.wait()


def flip_kernel(C, w_ref, out_ref):
    for tap in range(27):
        out_ref[tap * C:(tap + 1) * C, :] = jnp.transpose(w_ref[tap * C:(tap + 1) * C, :])


def back_conv(dm, t, pg, xf, x27, wt_ref, b_ref, msg_ref):
    width = dm.own + 2 * (t - 1)
    stage(xf, pg, dm.rows_of(t))
    spread(dm, xf, x27, width, -1)
    grad = dot(x27[0:width * dm.G, :], wt_ref[...])
    if t <= dm.half:
        grad = grad + dot_nt(pg[dm.G:dm.G + width * dm.G], b_ref[...])
    msg_ref[0:width * dm.G, :] = grad.astype(BF)


def flat_labels(dm, base, width, lab_ref):
    G, cells = dm.G, width * dm.G
    lanes = dm.C
    cell = lax.broadcasted_iota(jnp.int32, (lanes, cells), 1)
    row = lax.broadcasted_iota(jnp.int32, (lanes, cells), 0)
    pick = jnp.where((cell // G + base == row) & (row < dm.W), 1.0, 0.0).astype(BF)
    found = dot(lab_ref[...].astype(BF), pick)
    g = lax.broadcasted_iota(jnp.int32, (G, cells), 1) % G
    row = lax.broadcasted_iota(jnp.int32, (G, cells), 0)
    line = jnp.sum(jnp.where(g == row, found, 0.0), axis=0, keepdims=True)
    return jnp.broadcast_to(line, (8, cells))


def affinity(dm, width, lab, off_ref):
    G, cells = dm.G, width * dm.G
    total = lab.shape[1]
    mid = lab[:, G:G + cells]
    row = lax.broadcasted_iota(jnp.int32, (8, cells), 0)
    g = lax.broadcasted_iota(jnp.int32, (8, cells), 1) % G
    d, r = g // dm.R, g % dm.R
    target = jnp.zeros((8, cells), F32)
    for j in range(dm.offs):
        dz, dy, dx = off_ref[j, 0], off_ref[j, 1], off_ref[j, 2]
        shift = G + dx * G + dz * dm.R + dy
        near = pltpu.roll(lab, lax.rem(2 * total - shift, total), 1)[:, 0:cells]
        inside = (d + dz >= 0) & (d + dz < dm.D) & (r + dy >= 0) & (r + dy < dm.R)
        same = inside & (near == mid) & (mid != 0.0) & (row == j)
        target = jnp.where(same, 1.0, target)
    return target


def last_kernel(dm, *refs):
    (me_ref, off_ref, x_ref, w_ref, b_ref, skip_ref, kept_ref, wt_ref, head_ref, lab_ref) = refs[:10]
    msg_ref, pgx_ref, skip_out, own_ref, xf, x27 = refs[10:]
    t = dm.sections - 1

    @pl.when(me_ref[2] == t)
    def _():
        base = me_ref[0] * dm.own
        G, C, own = dm.G, dm.C, dm.own
        mid, size = t * G, own * G
        own_ref[...] = x_ref[mid + G:mid + G + size, :]
        stage(xf, x_ref[...], dm.rows_of(t + 1))
        pre = preact(dm, t, xf, x27, skip_ref, w_ref, b_ref)
        y = silu_masked(dm, base, t, pre)
        logits = dot_nt(head_ref[...], y)
        lab = flat_labels(dm, base - t - 1, own + 2 * t + 2, lab_ref)
        target = affinity(dm, own + 2 * t, lab, off_ref)
        live = lax.broadcasted_iota(jnp.int32, logits.shape, 0) < dm.offs
        sig = 1.0 / (1.0 + jnp.exp(-logits))
        lg = jnp.where(live, loss_scale * (sig - target) / dm.count, 0.0).astype(BF)
        term = jnp.maximum(logits, 0.0) + jnp.log(1.0 + jnp.exp(-jnp.abs(logits))) - target * logits
        term = jnp.where(live, term, 0.0)[:, mid:mid + size]
        loss = jnp.sum(jnp.sum(term, axis=1, keepdims=True), axis=0, keepdims=True)
        head_part = dot(lg[:, mid:mid + size], y[mid:mid + size])
        row = lax.broadcasted_iota(jnp.int32, (8, C), 0)
        carry = jnp.where(row < dm.offs, head_part, jnp.where(row == dm.offs, loss, 0.0))
        pieces = []
        for _ in range(3):
            piece = carry.astype(BF).astype(F32)
            pieces.append(piece)
            carry = carry - piece
        carry = jnp.concatenate(pieces + [jnp.zeros((8, C), F32)], axis=0).astype(BF)
        upstream = dot_tn(lg, head_ref[...])
        pg = pre_gradient(dm, base, t, upstream, pre)
        pgx_ref[0:size, :] = pg[mid:mid + size]
        pgx_ref[size:size + 32, :] = carry
        back_conv(dm, t, pg, xf, x27, wt_ref, b_ref, msg_ref)
        end = dm.rows_of(t - 1)
        msg_ref[end:end + 32, :] = carry
        m = dm.sections - 1 - t
        first = (t - m) * G
        skip_out[...] = dot_nt(pg[first:first + dm.rows_of(m)], b_ref[...]).astype(BF)

    @pl.when(me_ref[2] != t)
    def _():
        own_ref[...] = kept_ref[...]


def backward_kernel(dm, t, has_skip_in, *refs):
    refs = list(refs)
    me_ref, down_ref, pre_ref, kept_ref = refs[:4]
    at = 4
    if t > 0:
        wt_ref, b_ref = refs[at:at + 2]
        at += 2
    if has_skip_in:
        skip_ref = refs[at]
        at += 1
    pgx_ref = refs[at]
    at += 1
    if t > 0:
        msg_ref = refs[at]
        at += 1
        if t > dm.half:
            skip_out = refs[at]
            at += 1
        xf, x27 = refs[at:at + 2]

    @pl.when(me_ref[2] == t)
    def _():
        base = me_ref[0] * dm.own
        ro = dm.rows_of(t)
        upstream = down_ref[0:ro, :].astype(F32)
        if has_skip_in:
            upstream = upstream + skip_ref[0:ro, :].astype(F32)
        pg = pre_gradient(dm, base, t, upstream, pre_ref[...])
        mid, size = t * dm.G, dm.own * dm.G
        carry = down_ref[ro:ro + 32, :]
        pgx_ref[0:size, :] = pg[mid:mid + size]
        pgx_ref[size:size + 32, :] = carry
        if t > 0:
            back_conv(dm, t, pg, xf, x27, wt_ref, b_ref, msg_ref)
            end = dm.rows_of(t - 1)
            msg_ref[end:end + 32, :] = carry
            if t > dm.half:
                m = dm.sections - 1 - t
                first = (t - m) * dm.G
                skip_out[...] = dot_nt(pg[first:first + dm.rows_of(m)], b_ref[...]).astype(BF)

    @pl.when(me_ref[2] != t)
    def _():
        pgx_ref[...] = kept_ref[...]


def turn_kernel(dm, *refs):
    q_ref = refs[0]
    x_refs = refs[1:1 + dm.slabs]
    b_refs = refs[1 + dm.slabs:1 + 2 * dm.slabs]
    xt_ref, bt_ref, xf = refs[1 + 2 * dm.slabs:]
    C, size = dm.C, dm.own * dm.G
    cells = dm.slabs * size
    for e in range(dm.micro):
        for r in range(dm.parts):
            block = e * dm.parts + r
            place = lax.rem(q_ref[0] + (dm.parts - r), dm.parts) + e * dm.parts
            at = pl.multiple_of(place * size, size)
            xf[pl.ds(PAD + at, size), :] = x_refs[block][...].astype(F32)

            @pl.when(q_ref[2] > dm.half)
            def _():
                bt_ref[:, pl.ds(at, size)] = jnp.transpose(b_refs[block][...])

    for kz in range(3):
        for ky in range(3):
            delta = (kz - 1) * dm.R + ky - 1
            part = xf[PAD + delta:PAD + delta + cells, :]
            if kz != 1 or ky != 1:
                part = part.reshape(cells // dm.G, dm.G, C)
                part = jnp.where(group_mask(dm, kz - 1, ky - 1), part, 0.0).reshape(cells, C)
            tap = kz * 3 + ky
            xt_ref[tap * C:(tap + 1) * C, :] = jnp.transpose(part.astype(BF))


def weight_kernel(dm, *refs):
    q_ref, xt_ref, bt_ref = refs[:3]
    blocks = refs[3:3 + dm.slabs]
    grad_ref, mix_ref, head_ref, loss_ref, full, held, sums, sems = refs[3 + dm.slabs:]
    G, C, W = dm.G, dm.C, dm.W
    size = dm.own * G
    span = (W + 2) * G
    cells = W * G
    for e in range(dm.micro):
        start = e * span
        full[start:start + G, :] = jnp.zeros((G, C), BF)
        full[start + (W + 1) * G:start + span, :] = jnp.zeros((G, C), BF)
        for r in range(dm.parts):
            block = blocks[e * dm.parts + r]
            place = lax.rem(q_ref[0] + (dm.parts - r), dm.parts)
            at = pl.multiple_of(start + G + place * size, 16)
            full[pl.ds(at, size), :] = block[0:size, :]
            carry = block[size:size + 32, :].astype(F32)
            slot = lax.rem(q_ref[1] + (dm.micro - e), dm.micro) * dm.parts + place
            sums[slot] = (carry[0:8] + carry[8:16]) + carry[16:24]

    def product(lhs_ref, row, count, kx):
        total = None
        for e in range(dm.micro):
            first = e * span + (2 - kx) * G
            one = dot(lhs_ref[row:row + count, e * cells:(e + 1) * cells], full[first:first + cells, :])
            total = one if total is None else total + one
        return total

    copies = []
    for step in range(27):
        kx, tap = step // 9, step % 9
        held[step] = product(xt_ref, tap * C, C, kx)
        copies.append(pltpu.make_async_copy(held.at[step], grad_ref.at[tap, kx], sems.at[step]))
        copies[step].start()

    @pl.when(q_ref[2] > dm.half)
    def _():
        mix_ref[...] = product(bt_ref, 0, C, 1)

    @pl.when(q_ref[2] <= dm.half)
    def _():
        mix_ref[...] = held[13]

    total = jnp.zeros((8, C), F32)
    for slot in range(dm.slabs):
        total = total + sums[slot]
    head_ref[...] = total[0:dm.offs]
    loss_ref[...] = total[dm.offs:dm.offs + 1, 0:1] / dm.count
    for copy in copies:
        copy.wait()


def whole():
    return pl.BlockSpec(memory_space=pltpu.VMEM)


def scalar():
    return pl.BlockSpec(memory_space=pltpu.SMEM)


def shape(rows, cols, kind):
    return jax.ShapeDtypeStruct((rows, cols), kind)


def nbytes(arrays):
    return sum(math.prod(a.shape) * jnp.dtype(a.dtype).itemsize for a in arrays)


def call(kernel, scalars, operands, outs, scratch, flops, places=None):
    moved = nbytes(operands) + nbytes(outs)
    room = moved + nbytes([a for a in scratch if a.dtype in (BF, F32)]) + SPARE
    return pl.pallas_call(
        kernel,
        out_shape=outs,
        in_specs=[scalar()] * len(scalars) + [whole()] * len(operands),
        out_specs=places or [whole()] * len(outs),
        scratch_shapes=scratch,
        compiler_params=pltpu.CompilerParams(vmem_limit_bytes=room),
        cost_estimate=pl.CostEstimate(flops=flops, bytes_accessed=moved, transcendentals=0),
    )(*scalars, *operands)


def conv_scratch(dm, rin, ro):
    return [
        pltpu.VMEM((rin + 2 * PAD, dm.C), F32),
        pltpu.VMEM((ro, 27 * dm.C), BF),
    ]


def body(features_in, labels, offsets, conv_weight, branch_weight, head_weight):
    n = lax.axis_size("section")
    slabs = lax.axis_size("slab")
    micro, C, thick, R, W = features_in.shape
    dm = Dims(n, slabs, micro, C, thick * slabs, R, W, offsets.shape[0])
    G, own, parts, half = dm.G, dm.own, dm.parts, dm.half
    section = lax.axis_index("section")
    slab = lax.axis_index("slab")
    c, q = lax.rem(slab, micro), lax.div(slab, micro)
    me = jnp.stack([q, c, section]).astype(jnp.int32)
    size = own * G

    def hop(x, source, target):
        return lax.ppermute(x, "section", [(source, target)])

    def rotate(x, r):
        pairs = [(p * micro + e, ((p + r) % parts) * micro + e) for p in range(parts) for e in range(micro)]
        return lax.ppermute(x, "slab", pairs)

    def swap(x, e):
        pairs = [(p * micro + i, p * micro + (i + e) % micro) for p in range(parts) for i in range(micro)]
        return lax.ppermute(x, "slab", pairs)

    def gather(block, lowest):
        found = [block]
        for r in range(1, parts):
            pairs = [(p * micro + e, (p + r) % parts * micro + e) for p in range(parts) for e in range(micro)]
            found.append(along(block, pairs, lowest))
        blocks = list(found)
        for e in range(1, micro):
            pairs = [(p * micro + i, p * micro + (i + e) % micro) for p in range(parts) for i in range(micro)]
            blocks += [along(b, pairs, lowest) for b in found]
        return blocks

    def along(x, pairs, lowest):
        joint = [(s * slabs + i, s * slabs + j) for s in range(lowest, n) for i, j in pairs]
        return lax.ppermute(x, ("section", "slab"), joint)

    source = conv_weight[0].reshape(27 * C, C)
    held_hbm = pl.BlockSpec(memory_space=pltpu.HBM)
    kernel, mixing = pl.pallas_call(
        functools.partial(load_kernel, 9),
        name="load",
        out_shape=[shape(27 * C, C, BF), shape(C, C, BF)],
        in_specs=[held_hbm, held_hbm],
        out_specs=[whole(), whole()],
        scratch_shapes=[pltpu.SemaphoreType.DMA((10,))],
        compiler_params=pltpu.CompilerParams(vmem_limit_bytes=27 * C * C * 2 + SPARE),
        cost_estimate=pl.CostEstimate(flops=0, bytes_accessed=27 * C * C * 4, transcendentals=0),
    )(source, branch_weight[0])

    wing = dm.fwd(0) + 1
    wide = own + 2 * wing
    cols = -(-(wide + 1) // 16) * 16
    cells = jnp.transpose(features_in, (0, 2, 3, 4, 1)).reshape(micro * thick * R, W, C)
    front = -(-wing // 8) * 8
    packs = call(
        functools.partial(pack_kernel, dm, wing, cols),
        [me], [cells, labels.reshape(micro * thick * R, W)],
        [shape(slabs * thick * R * cols, C, BF)],
        [
            pltpu.VMEM((front + W + cols, C), F32),
            pltpu.VMEM((-(-micro * thick * R // 8) * 8, C), F32),
        ],
        1000,
    )[0].reshape(slabs, thick * R, cols, C)
    first = lax.all_to_all(packs, "slab", 0, 0, tiled=True).reshape(G, cols, C)
    current = first

    head = jnp.pad(jnp.transpose(head_weight), ((0, 8 - dm.offs), (0, 0)))

    pres, mirrors = [], {}
    kept = kernel_t = None
    for t in range(n - 1):
        k = dm.fwd(t)
        has_skip, has_mirror = t > half, t < half - 1
        operands = [current, kernel, mixing]
        if has_skip:
            operands.append(mirrors[t])
        if t > 0:
            operands.append(kept)
        outs = [shape(dm.rows_of(k), C, BF), shape(dm.rows_of(t), C, F32), shape(size, C, BF)]
        scratch = conv_scratch(dm, dm.rows_of(k + 1), dm.rows_of(k))
        if has_mirror:
            outs.append(shape(dm.rows_of(dm.fwd(n - 1 - t)), C, BF))
        if t == 0:
            outs.append(shape(G, C, F32))
        results = call(
            functools.partial(forward_kernel, dm, t, has_skip, has_mirror),
            [me], operands, outs, scratch,
            2 * dm.rows_of(k) * 28 * C * C,
        )
        pres.append(results[1])
        kept = results[2]
        current = hop(results[0], t, t + 1)
        if t == 0:
            marks = results[-1]
            raw, _ = lax.optimization_barrier((kernel, results[0]))
            kernel_t = call(
                functools.partial(flip_kernel, C), [], [raw],
                [shape(27 * C, C, BF)], [], 2 * 27 * C * C * 100,
            )[0]
        if has_mirror:
            later, current = lax.optimization_barrier((results[3], current))
            mirrors[n - 1 - t] = hop(later, t, n - 1 - t)

    t = n - 1
    skip = mirrors[t]
    branch = skip[t * G:t * G + size]
    for s in range(half + 1, n - 1):
        first = dm.fwd(s) * G
        branch = jnp.where(section == s, mirrors[s][first:first + size], branch)
    branch, _ = lax.optimization_barrier((branch, results[0]))
    branches = gather(branch, half + 1)
    outs = [
        shape(dm.rows_of(t - 1) + 32, C, BF),
        shape(size + 32, C, BF),
        shape(dm.rows_of(0), C, BF),
        shape(size, C, BF),
    ]
    results = call(
        functools.partial(last_kernel, dm),
        [me, offsets],
        [current, kernel, mixing, skip, kept, kernel_t, head, marks],
        outs,
        conv_scratch(dm, dm.rows_of(t + 1), dm.rows_of(t)),
        4 * dm.rows_of(t) * 28 * C * C,
    )
    down = hop(results[0], t, t - 1)
    block, held = results[1], results[3]
    skip_grads = {0: hop(results[2], t, 0)}
    held = gather(held, 0)
    cells_all = micro * W * G

    for t in range(n - 2, -1, -1):
        has_skip = t < half - 1
        operands = [down, pres[t], block]
        if t > 0:
            operands += [kernel_t, mixing]
        if has_skip:
            operands.append(skip_grads[t])
        outs = [shape(size + 32, C, BF)]
        scratch = []
        if t > 0:
            outs.append(shape(dm.rows_of(t - 1) + 32, C, BF))
            if t > half:
                outs.append(shape(dm.rows_of(n - 1 - t), C, BF))
            scratch = conv_scratch(dm, dm.rows_of(t), dm.rows_of(t - 1))
        results = call(
            functools.partial(backward_kernel, dm, t, has_skip),
            [me], operands, outs, scratch,
            2 * dm.rows_of(max(t - 1, 0)) * 28 * C * C if t > 0 else 1000,
        )
        block = results[0]
        if t > 0:
            down = hop(results[1], t, t - 1)
            if t > half:
                skip_grads[n - 1 - t] = hop(results[2], t, n - 1 - t)

    held[0], _ = lax.optimization_barrier((held[0], block))
    xt, bt = call(
        functools.partial(turn_kernel, dm),
        [me], held + branches,
        [shape(9 * C, cells_all, BF), shape(C, cells_all, BF)],
        [pltpu.VMEM((cells_all + 2 * PAD, C), F32)],
        2 * 10 * cells_all * C * 100,
    )
    near = [block] + [rotate(block, r) for r in range(1, parts)]
    *far, xt = lax.optimization_barrier((*near[1:], xt))
    near = [block] + far
    blocks = list(near)
    for e in range(1, micro):
        blocks += [swap(b, e) for b in near]
    operands = [xt, bt, *blocks]
    scratch = [
        pltpu.VMEM((micro * (W + 2) * G, C), BF),
        pltpu.VMEM((27, C, C), F32),
        pltpu.VMEM((slabs, 8, C), F32),
        pltpu.SemaphoreType.DMA((27,)),
    ]
    outs = [
        jax.ShapeDtypeStruct((9, 3, C, C), F32),
        shape(C, C, F32),
        shape(dm.offs, C, F32),
        shape(1, 1, F32),
    ]
    moved = nbytes(operands) + nbytes(outs)
    grad, mix, heads, loss = pl.pallas_call(
        functools.partial(weight_kernel, dm),
        name="weights",
        out_shape=outs,
        in_specs=[scalar()] + [whole()] * len(operands),
        out_specs=[pl.BlockSpec(memory_space=pl.ANY), whole(), whole(), whole()],
        scratch_shapes=scratch,
        compiler_params=pltpu.CompilerParams(
            vmem_limit_bytes=nbytes(operands) + nbytes(scratch[:3]) + SPARE
        ),
        cost_estimate=pl.CostEstimate(
            flops=2 * cells_all * 28 * C * C, bytes_accessed=moved, transcendentals=0
        ),
    )(me, *operands)
    return (
        loss[0, 0],
        grad.reshape((1, 3, 3, 3, C, C)),
        mix[None],
        jnp.transpose(heads),
    )


def solution(mesh):
    placed = (
        P(None, None, "slab", None, None),
        P(None, "slab", None, None),
        P(),
        P("section", None, None, None, None, None),
        P("section", None, None),
        P(),
    )
    return jax.shard_map(
        body,
        mesh=mesh,
        in_specs=placed,
        out_specs=(P(), P("section", None, None, None, None, None), P("section", None, None), P()),
        check_vma=False,
    )
```

```python
import functools
import math

import jax
import jax.numpy as jnp
from jax import lax
from jax.experimental import pallas as pl
from jax.experimental.pallas import tpu as pltpu
from jax.sharding import PartitionSpec as P


loss_scale = 1024.0
BF = jnp.bfloat16
F32 = jnp.float32
PAD = 8
SPARE = 6 * 1024 * 1024
CARRY = 16


class Dims:
    def __init__(self, sections, slabs, micro, channels, depth, rows, cols, offs):
        self.sections, self.half = sections, sections // 2
        self.slabs, self.micro = slabs, micro
        self.C, self.D, self.R, self.W, self.offs = channels, depth, rows, cols, offs
        self.G = depth * rows
        self.parts = slabs // micro
        self.own = cols // self.parts
        self.count = micro * offs * depth * rows * cols

    def fwd(self, t):
        return 2 * (self.sections - 1) - t

    def rows_of(self, k):
        return (self.own + 2 * k) * self.G


def group_mask(dm, kz, ky):
    g = lax.broadcasted_iota(jnp.int32, (1, dm.G, dm.C), 1)
    d = g // dm.R + kz
    r = g % dm.R + ky
    return (d >= 0) & (d < dm.D) & (r >= 0) & (r < dm.R)


def column_mask(dm, base, k, width):
    col = lax.broadcasted_iota(jnp.int32, (width, dm.G, dm.C), 0) + (base - k)
    return (col >= 0) & (col < dm.W)


def spread(dm, xf, x27, width, sign):
    G, C = dm.G, dm.C
    rin = (width + 2) * G
    for kz in range(3):
        for ky in range(3):
            dz, dy = sign * (kz - 1), sign * (ky - 1)
            delta = dz * dm.R + dy
            part = xf[PAD + delta:PAD + delta + rin, :]
            if kz != 1 or ky != 1:
                part = part.reshape(width + 2, G, C)
                part = jnp.where(group_mask(dm, dz, dy), part, 0.0).reshape(rin, C)
            part = part.astype(BF)
            for kx in range(3):
                first = (1 + sign * (kx - 1)) * G
                tap = (kz * 3 + ky) * 3 + kx
                x27[0:width * G, tap * C:(tap + 1) * C] = part[first:first + width * G]


def dot(a, b):
    return lax.dot_general(a, b, (((1,), (0,)), ((), ())), preferred_element_type=F32)


def dot_nt(a, b):
    return lax.dot_general(a, b, (((1,), (1,)), ((), ())), preferred_element_type=F32)


def dot_tn(a, b):
    return lax.dot_general(a, b, (((0,), (0,)), ((), ())), preferred_element_type=F32)


def stage(xf, x, rin):
    xf[PAD:PAD + rin, :] = x.astype(F32)


def preact(dm, t, xf, x27, skip_ref, w_ref, b_ref):
    width = dm.own + 2 * dm.fwd(t)
    ro = width * dm.G
    spread(dm, xf, x27, width, 1)
    if t <= dm.half:
        branch = x27[0:ro, 13 * dm.C:14 * dm.C]
    else:
        branch = skip_ref[0:ro, :]
    return dot(x27[0:ro, :], w_ref[...]) + dot(branch, b_ref[...])


def silu_masked(dm, base, k, pre):
    width = dm.own + 2 * k
    value = pre * (1.0 / (1.0 + jnp.exp(-pre)))
    value = value.reshape(width, dm.G, dm.C)
    value = jnp.where(column_mask(dm, base, k, width), value, 0.0)
    return value.reshape(width * dm.G, dm.C).astype(BF)


def pre_gradient(dm, base, k, upstream, pre):
    width = dm.own + 2 * k
    sig = 1.0 / (1.0 + jnp.exp(-pre))
    value = upstream * (sig * (1.0 + pre * (1.0 - sig)))
    value = value.reshape(width, dm.G, dm.C)
    value = jnp.where(column_mask(dm, base, k, width), value, 0.0)
    return value.reshape(width * dm.G, dm.C).astype(BF)


def forward_kernel(dm, t, has_skip_in, has_mirror, *refs):
    refs = list(refs)
    count = dm.parts if t == 0 else 1
    me_ref, x_refs = refs[0], refs[1:1 + count]
    w_ref, b_ref = refs[1 + count:3 + count]
    at = 3 + count
    x_ref = x_refs[0]
    skip_ref = kept_ref = None
    if has_skip_in:
        skip_ref = refs[at]
        at += 1
    if t > 0:
        kept_ref = refs[at]
        at += 1
    y_ref, pre_ref, own_ref = refs[at:at + 3]
    at += 3
    if has_mirror:
        mirror_ref = refs[at]
        at += 1
    if t == 0:
        lab_ref, xg = refs[at], refs[-1]
        at += 1
        wide = dm.own + 2 * (dm.fwd(0) + 1)
        layers = dm.G // dm.parts
        for r in range(dm.parts):
            place = lax.rem(me_ref[0] + (dm.parts - r), dm.parts)
            xg[pl.ds(place * layers, layers)] = x_refs[r][...].astype(F32)
        lab_ref[...] = xg[:, wide, :]
    xf, x27 = refs[at:at + 2]

    @pl.when(me_ref[2] == t)
    def _():
        base = me_ref[0] * dm.own
        k = dm.fwd(t)
        if t == 0:
            gather_cells(dm, xg, xf)
        else:
            stage(xf, x_ref[...], dm.rows_of(k + 1))
        size, mid = dm.own * dm.G, (k + 1) * dm.G
        own_ref[...] = xf[PAD + mid:PAD + mid + size, :].astype(BF)
        pre = preact(dm, t, xf, x27, skip_ref, w_ref, b_ref)
        first = (k - t) * dm.G
        pre_ref[...] = pre[first:first + dm.rows_of(t)]
        y = silu_masked(dm, base, k, pre)
        y_ref[...] = y
        if has_mirror:
            keep = dm.fwd(dm.sections - 1 - t)
            first = (k - keep) * dm.G
            mirror_ref[...] = y[first:first + dm.rows_of(keep)]

    if t > 0:
        @pl.when(me_ref[2] != t)
        def _():
            own_ref[...] = kept_ref[...]


def split_kernel(dm, me_ref, f_ref, l_ref, *refs):
    outs, marks = refs[:dm.micro], refs[dm.micro]
    W = dm.W
    layers = f_ref.shape[0] // dm.micro
    for e in range(dm.micro):
        crop = lax.rem(me_ref[1] + e, dm.micro)
        marks[...] = jnp.zeros(marks.shape, F32)
        for layer in range(layers):
            at = crop * layers + layer
            outs[e][layer * W:(layer + 1) * W, :] = f_ref[at]
            marks[layer:layer + 1, 0:W] = l_ref[at].astype(F32)
        outs[e][layers * W:, :] = marks[...].astype(BF)


def window_kernel(dm, wing, cols, me_ref, *refs):
    crops, outs, xs = refs[:dm.micro], refs[dm.micro:-1], refs[-1]
    C, W, own = dm.C, dm.W, dm.own
    layers = dm.G // dm.slabs
    xs[0:16, :] = jnp.zeros((16, C), F32)
    xs[wing + W:, :] = jnp.zeros((xs.shape[0] - wing - W, C), F32)
    row = lax.broadcasted_iota(jnp.int32, (cols, C), 0)
    for e in range(dm.micro):
        crop = crops[e][...].astype(F32)
        core = lax.rem(me_ref[1] + (dm.micro - e), dm.micro)
        for layer in range(layers):
            xs[wing:wing + W, :] = crop[layer * W:(layer + 1) * W]
            mark = crop[layers * W + layer:layers * W + layer + 1]
            for r in range(dm.parts):
                place = lax.rem(me_ref[0] + r, dm.parts)
                start = pl.multiple_of(place * own, 8)
                value = jnp.where(row == own + 2 * wing, mark, xs[pl.ds(start, cols), :])
                outs[r][core * layers + layer] = value.astype(BF)


def gather_cells(dm, xg, xf):
    rows = (dm.own + 2 * (dm.fwd(0) + 1)) * dm.G
    cells = jnp.transpose(xg[...], (1, 0, 2))
    cells = cells.reshape(cells.shape[0] * dm.G, dm.C)
    xf[PAD:PAD + rows, :] = cells[0:rows]


def load_kernel(chunks, w_ref, b_ref, out_ref, out_b_ref, sems):
    rows = w_ref.shape[0] // chunks
    copies = []
    for i in range(chunks):
        part = pl.ds(i * rows, rows)
        copies.append(pltpu.make_async_copy(w_ref.at[part], out_ref.at[part], sems.at[i]))
        copies[i].start()
    copies.append(pltpu.make_async_copy(b_ref, out_b_ref, sems.at[chunks]))
    copies[chunks].start()
    for copy in copies:
        copy.wait()


def flip_kernel(C, w_ref, out_ref):
    for tap in range(27):
        out_ref[tap * C:(tap + 1) * C, :] = jnp.transpose(w_ref[tap * C:(tap + 1) * C, :])


def back_conv(dm, t, pg, xf, x27, wt_ref, b_ref, msg_ref):
    width = dm.own + 2 * (t - 1)
    stage(xf, pg, dm.rows_of(t))
    spread(dm, xf, x27, width, -1)
    grad = dot(x27[0:width * dm.G, :], wt_ref[...])
    if t <= dm.half:
        grad = grad + dot_nt(pg[dm.G:dm.G + width * dm.G], b_ref[...])
    msg_ref[0:width * dm.G, :] = grad.astype(BF)


def flat_labels(dm, base, width, lab_ref):
    G, cells = dm.G, width * dm.G
    lanes = dm.C
    cell = lax.broadcasted_iota(jnp.int32, (lanes, cells), 1)
    row = lax.broadcasted_iota(jnp.int32, (lanes, cells), 0)
    pick = jnp.where((cell // G + base == row) & (row < dm.W), 1.0, 0.0).astype(BF)
    found = dot(lab_ref[...].astype(BF), pick)
    g = lax.broadcasted_iota(jnp.int32, (G, cells), 1) % G
    row = lax.broadcasted_iota(jnp.int32, (G, cells), 0)
    line = jnp.sum(jnp.where(g == row, found, 0.0), axis=0, keepdims=True)
    return jnp.broadcast_to(line, (8, cells))


def affinity(dm, width, lab, off_ref):
    G, cells = dm.G, width * dm.G
    total = lab.shape[1]
    mid = lab[:, G:G + cells]
    row = lax.broadcasted_iota(jnp.int32, (8, cells), 0)
    g = lax.broadcasted_iota(jnp.int32, (8, cells), 1) % G
    d, r = g // dm.R, g % dm.R
    target = jnp.zeros((8, cells), F32)
    for j in range(dm.offs):
        dz, dy, dx = off_ref[j, 0], off_ref[j, 1], off_ref[j, 2]
        shift = G + dx * G + dz * dm.R + dy
        near = pltpu.roll(lab, lax.rem(2 * total - shift, total), 1)[:, 0:cells]
        inside = (d + dz >= 0) & (d + dz < dm.D) & (r + dy >= 0) & (r + dy < dm.R)
        same = inside & (near == mid) & (mid != 0.0) & (row == j)
        target = jnp.where(same, 1.0, target)
    return target


def target_kernel(dm, me_ref, off_ref, lab_ref, out_ref):
    t = dm.sections - 1
    lab = flat_labels(dm, me_ref[0] * dm.own - t - 1, dm.own + 2 * t + 2, lab_ref)
    out_ref[...] = affinity(dm, dm.own + 2 * t, lab, off_ref)


def last_kernel(dm, *refs):
    (me_ref, x_ref, w_ref, b_ref, skip_ref, kept_ref, wt_ref, head_ref, target_ref) = refs[:9]
    msg_ref, pgx_ref, skip_out, own_ref, xf, x27, lines = refs[9:]
    t = dm.sections - 1

    @pl.when(me_ref[2] == t)
    def _():
        base = me_ref[0] * dm.own
        G, C, own = dm.G, dm.C, dm.own
        mid, size = t * G, own * G
        own_ref[...] = x_ref[mid + G:mid + G + size, :]
        stage(xf, x_ref[...], dm.rows_of(t + 1))
        pre = preact(dm, t, xf, x27, skip_ref, w_ref, b_ref)
        y = silu_masked(dm, base, t, pre)
        logits = dot_nt(head_ref[...], y)
        target = target_ref[...]
        live = lax.broadcasted_iota(jnp.int32, logits.shape, 0) < dm.offs
        sig = 1.0 / (1.0 + jnp.exp(-logits))
        lg = jnp.where(live, loss_scale * (sig - target) / dm.count, 0.0).astype(BF)
        term = jnp.maximum(logits, 0.0) + jnp.log(1.0 + jnp.exp(-jnp.abs(logits))) - target * logits
        term = jnp.where(live, term, 0.0)[:, mid:mid + size]
        loss = jnp.sum(jnp.sum(term, axis=1, keepdims=True), axis=0, keepdims=True)
        head_part = dot(lg[:, mid:mid + size], y[mid:mid + size])
        used = dm.offs + 1
        lines[...] = jnp.zeros(lines.shape, F32)
        lines[0:dm.offs, :] = head_part[0:dm.offs]
        lines[dm.offs:used, :] = jnp.broadcast_to(loss, (1, C))
        rest = lines[0:8, :]
        for i in range(3):
            piece = rest.astype(BF).astype(F32)
            lines[i * used:(i + 1) * used, :] = piece[0:used]
            rest = rest - piece
        carry = lines[...].astype(BF)
        upstream = dot_tn(lg, head_ref[...])
        pg = pre_gradient(dm, base, t, upstream, pre)
        pgx_ref[0:size, :] = pg[mid:mid + size]
        pgx_ref[size:size + CARRY, :] = carry
        back_conv(dm, t, pg, xf, x27, wt_ref, b_ref, msg_ref)
        end = dm.rows_of(t - 1)
        msg_ref[end:end + CARRY, :] = carry
        m = dm.sections - 1 - t
        first = (t - m) * G
        skip_out[...] = dot_nt(pg[first:first + dm.rows_of(m)], b_ref[...]).astype(BF)

    @pl.when(me_ref[2] != t)
    def _():
        own_ref[...] = kept_ref[...]


def backward_kernel(dm, t, has_skip_in, *refs):
    refs = list(refs)
    me_ref, down_ref, pre_ref, kept_ref = refs[:4]
    at = 4
    if t > 0:
        wt_ref, b_ref = refs[at:at + 2]
        at += 2
    if has_skip_in:
        skip_ref = refs[at]
        at += 1
    pgx_ref = refs[at]
    at += 1
    if t > 0:
        msg_ref = refs[at]
        at += 1
        if t > dm.half:
            skip_out = refs[at]
            at += 1
        xf, x27 = refs[at:at + 2]

    @pl.when(me_ref[2] == t)
    def _():
        base = me_ref[0] * dm.own
        ro = dm.rows_of(t)
        upstream = down_ref[0:ro, :].astype(F32)
        if has_skip_in:
            upstream = upstream + skip_ref[0:ro, :].astype(F32)
        pg = pre_gradient(dm, base, t, upstream, pre_ref[...])
        mid, size = t * dm.G, dm.own * dm.G
        carry = down_ref[ro:ro + CARRY, :]
        pgx_ref[0:size, :] = pg[mid:mid + size]
        pgx_ref[size:size + CARRY, :] = carry
        if t > 0:
            back_conv(dm, t, pg, xf, x27, wt_ref, b_ref, msg_ref)
            end = dm.rows_of(t - 1)
            msg_ref[end:end + CARRY, :] = carry
            if t > dm.half:
                m = dm.sections - 1 - t
                first = (t - m) * dm.G
                skip_out[...] = dot_nt(pg[first:first + dm.rows_of(m)], b_ref[...]).astype(BF)

    @pl.when(me_ref[2] != t)
    def _():
        pgx_ref[...] = kept_ref[...]


def turn_kernel(dm, *refs):
    q_ref = refs[0]
    x_refs = refs[1:1 + dm.slabs]
    b_refs = refs[1 + dm.slabs:1 + 2 * dm.slabs]
    xt_ref, bt_ref, xf = refs[1 + 2 * dm.slabs:]
    C, size = dm.C, dm.own * dm.G
    cells = dm.slabs * size
    for e in range(dm.micro):
        for r in range(dm.parts):
            block = e * dm.parts + r
            place = lax.rem(q_ref[0] + (dm.parts - r), dm.parts) + e * dm.parts
            at = pl.multiple_of(place * size, size)
            xf[pl.ds(PAD + at, size), :] = x_refs[block][...].astype(F32)

            @pl.when(q_ref[2] > dm.half)
            def _():
                bt_ref[:, pl.ds(at, size)] = jnp.transpose(b_refs[block][...])

    for kz in range(3):
        for ky in range(3):
            delta = (kz - 1) * dm.R + ky - 1
            part = xf[PAD + delta:PAD + delta + cells, :]
            if kz != 1 or ky != 1:
                part = part.reshape(cells // dm.G, dm.G, C)
                part = jnp.where(group_mask(dm, kz - 1, ky - 1), part, 0.0).reshape(cells, C)
            tap = kz * 3 + ky
            xt_ref[tap * C:(tap + 1) * C, :] = jnp.transpose(part.astype(BF))


def weight_kernel(dm, *refs):
    q_ref, xt_ref, bt_ref = refs[:3]
    blocks = refs[3:3 + dm.slabs]
    grad_ref, mix_ref, head_ref, loss_ref, full, held, sums, sems = refs[3 + dm.slabs:]
    G, C, W = dm.G, dm.C, dm.W
    size = dm.own * G
    span = (W + 2) * G
    cells = W * G
    for e in range(dm.micro):
        start = e * span
        full[start:start + G, :] = jnp.zeros((G, C), BF)
        full[start + (W + 1) * G:start + span, :] = jnp.zeros((G, C), BF)
        for r in range(dm.parts):
            block = blocks[e * dm.parts + r]
            place = lax.rem(q_ref[0] + (dm.parts - r), dm.parts)
            at = pl.multiple_of(start + G + place * size, 16)
            full[pl.ds(at, size), :] = block[0:size, :]
            carry = block[size:size + CARRY, :].astype(F32)
            slot = lax.rem(q_ref[1] + (dm.micro - e), dm.micro) * dm.parts + place
            used = dm.offs + 1
            sums[slot, 0:used] = (carry[0:used] + carry[used:2 * used]) + carry[2 * used:3 * used]

    def product(lhs_ref, row, count, kx):
        total = None
        for e in range(dm.micro):
            first = e * span + (2 - kx) * G
            one = dot(lhs_ref[row:row + count, e * cells:(e + 1) * cells], full[first:first + cells, :])
            total = one if total is None else total + one
        return total

    copies = []
    for step in range(27):
        kx, tap = step // 9, step % 9
        held[step] = product(xt_ref, tap * C, C, kx)
        copies.append(pltpu.make_async_copy(held.at[step], grad_ref.at[tap, kx], sems.at[step]))
        copies[step].start()

    @pl.when(q_ref[2] > dm.half)
    def _():
        mix_ref[...] = product(bt_ref, 0, C, 1)

    @pl.when(q_ref[2] <= dm.half)
    def _():
        mix_ref[...] = held[13]

    total = jnp.zeros((8, C), F32)
    for slot in range(dm.slabs):
        total = total + sums[slot]
    head_ref[...] = total[0:dm.offs]
    loss_ref[...] = total[dm.offs:dm.offs + 1, 0:1] / dm.count
    for copy in copies:
        copy.wait()


def whole():
    return pl.BlockSpec(memory_space=pltpu.VMEM)


def scalar():
    return pl.BlockSpec(memory_space=pltpu.SMEM)


def shape(rows, cols, kind):
    return jax.ShapeDtypeStruct((rows, cols), kind)


def nbytes(arrays):
    return sum(math.prod(a.shape) * jnp.dtype(a.dtype).itemsize for a in arrays)


def call(kernel, scalars, operands, outs, scratch, flops, places=None):
    moved = nbytes(operands) + nbytes(outs)
    room = moved + nbytes([a for a in scratch if a.dtype in (BF, F32)]) + SPARE
    return pl.pallas_call(
        kernel,
        out_shape=outs,
        in_specs=[scalar()] * len(scalars) + [whole()] * len(operands),
        out_specs=places or [whole()] * len(outs),
        scratch_shapes=scratch,
        compiler_params=pltpu.CompilerParams(vmem_limit_bytes=room),
        cost_estimate=pl.CostEstimate(flops=flops, bytes_accessed=moved, transcendentals=0),
    )(*scalars, *operands)


def conv_scratch(dm, rin, ro):
    return [
        pltpu.VMEM((rin + 2 * PAD, dm.C), F32),
        pltpu.VMEM((ro, 27 * dm.C), BF),
    ]


def body(features_in, labels, offsets, conv_weight, branch_weight, head_weight):
    n = lax.axis_size("section")
    slabs = lax.axis_size("slab")
    micro, C, thick, R, W = features_in.shape
    dm = Dims(n, slabs, micro, C, thick * slabs, R, W, offsets.shape[0])
    G, own, parts, half = dm.G, dm.own, dm.parts, dm.half
    section = lax.axis_index("section")
    slab = lax.axis_index("slab")
    c, q = lax.rem(slab, micro), lax.div(slab, micro)
    me = jnp.stack([q, c, section]).astype(jnp.int32)
    size = own * G

    def hop(x, source, target):
        return lax.ppermute(x, "section", [(source, target)])

    def rotate(x, r):
        pairs = [(p * micro + e, ((p + r) % parts) * micro + e) for p in range(parts) for e in range(micro)]
        return lax.ppermute(x, "slab", pairs)

    def swap(x, e):
        pairs = [(p * micro + i, p * micro + (i + e) % micro) for p in range(parts) for i in range(micro)]
        return lax.ppermute(x, "slab", pairs)

    def gather(block, lowest):
        found = [block]
        for r in range(1, parts):
            pairs = [(p * micro + e, (p + r) % parts * micro + e) for p in range(parts) for e in range(micro)]
            found.append(along(block, pairs, lowest))
        blocks = list(found)
        for e in range(1, micro):
            pairs = [(p * micro + i, p * micro + (i + e) % micro) for p in range(parts) for i in range(micro)]
            blocks += [along(b, pairs, lowest) for b in found]
        return blocks

    def along(x, pairs, lowest):
        joint = [(s * slabs + i, s * slabs + j) for s in range(lowest, n) for i, j in pairs]
        return lax.ppermute(x, ("section", "slab"), joint)

    source = conv_weight[0].reshape(27 * C, C)
    held_hbm = pl.BlockSpec(memory_space=pltpu.HBM)
    kernel, mixing = pl.pallas_call(
        functools.partial(load_kernel, 9),
        name="load",
        out_shape=[shape(27 * C, C, BF), shape(C, C, BF)],
        in_specs=[held_hbm, held_hbm],
        out_specs=[whole(), whole()],
        scratch_shapes=[pltpu.SemaphoreType.DMA((10,))],
        compiler_params=pltpu.CompilerParams(vmem_limit_bytes=27 * C * C * 2 + SPARE),
        cost_estimate=pl.CostEstimate(flops=0, bytes_accessed=27 * C * C * 4, transcendentals=0),
    )(source, branch_weight[0])

    wing = dm.fwd(0) + 1
    wide = own + 2 * wing
    cols = -(-(wide + 1) // 16) * 16
    layers = thick * R
    cells = jnp.transpose(features_in, (0, 2, 3, 4, 1)).reshape(micro * layers, W, C)
    lines = -(-layers // 16) * 16
    crops = list(call(
        functools.partial(split_kernel, dm),
        [me], [cells, labels.reshape(micro * layers, 1, W)],
        [shape(layers * W + lines, C, BF)] * micro,
        [pltpu.VMEM((lines, C), F32)],
        1000,
    ))
    for e in range(1, micro):
        crops[e] = swap(crops[e], e)
    windows = call(
        functools.partial(window_kernel, dm, wing, cols),
        [me], crops,
        [jax.ShapeDtypeStruct((micro * layers, cols, C), BF)] * parts,
        [pltpu.VMEM((-(-(wing + W + cols) // 8) * 8, C), F32)],
        1000,
    )
    current = [windows[0]]
    for r in range(1, parts):
        current.append(rotate(windows[r], r))

    head = jnp.pad(jnp.transpose(head_weight), ((0, 8 - dm.offs), (0, 0)))

    pres, mirrors = [], {}
    kept = kernel_t = None
    for t in range(n - 1):
        k = dm.fwd(t)
        has_skip, has_mirror = t > half, t < half - 1
        operands = [*(current if t == 0 else [current]), kernel, mixing]
        if has_skip:
            operands.append(mirrors[t])
        if t > 0:
            operands.append(kept)
        outs = [shape(dm.rows_of(k), C, BF), shape(dm.rows_of(t), C, F32), shape(size, C, BF)]
        scratch = conv_scratch(dm, dm.rows_of(k + 1), dm.rows_of(k))
        if has_mirror:
            outs.append(shape(dm.rows_of(dm.fwd(n - 1 - t)), C, BF))
        if t == 0:
            outs.append(shape(G, C, F32))
            scratch.append(pltpu.VMEM((G, cols, C), F32))
        results = call(
            functools.partial(forward_kernel, dm, t, has_skip, has_mirror),
            [me], operands, outs, scratch,
            2 * dm.rows_of(k) * 28 * C * C,
        )
        pres.append(results[1])
        kept = results[2]
        current = hop(results[0], t, t + 1)
        if t == 0:
            marks = results[-1]
            raw, marks, _ = lax.optimization_barrier((kernel, marks, results[0]))
            targets = call(
                functools.partial(target_kernel, dm), [me, offsets], [marks],
                [shape(8, dm.rows_of(n - 1), F32)], [], 1000,
            )[0]
            kernel_t = call(
                functools.partial(flip_kernel, C), [], [raw],
                [shape(27 * C, C, BF)], [], 2 * 27 * C * C * 100,
            )[0]
        if has_mirror:
            later, current = lax.optimization_barrier((results[3], current))
            mirrors[n - 1 - t] = hop(later, t, n - 1 - t)

    t = n - 1
    skip = mirrors[t]
    branch = skip[t * G:t * G + size]
    for s in range(half + 1, n - 1):
        first = dm.fwd(s) * G
        branch = jnp.where(section == s, mirrors[s][first:first + size], branch)
    branch, _ = lax.optimization_barrier((branch, results[0]))
    branches = gather(branch, half + 1)
    outs = [
        shape(dm.rows_of(t - 1) + CARRY, C, BF),
        shape(size + CARRY, C, BF),
        shape(dm.rows_of(0), C, BF),
        shape(size, C, BF),
    ]
    results = call(
        functools.partial(last_kernel, dm),
        [me],
        [current, kernel, mixing, skip, kept, kernel_t, head, targets],
        outs,
        conv_scratch(dm, dm.rows_of(t + 1), dm.rows_of(t)) + [pltpu.VMEM((CARRY, C), F32)],
        4 * dm.rows_of(t) * 28 * C * C,
    )
    down = hop(results[0], t, t - 1)
    block, held = results[1], results[3]
    skip_grads = {0: hop(results[2], t, 0)}
    held = gather(held, 0)
    cells_all = micro * W * G

    for t in range(n - 2, -1, -1):
        has_skip = t < half - 1
        operands = [down, pres[t], block]
        if t > 0:
            operands += [kernel_t, mixing]
        if has_skip:
            operands.append(skip_grads[t])
        outs = [shape(size + CARRY, C, BF)]
        scratch = []
        if t > 0:
            outs.append(shape(dm.rows_of(t - 1) + CARRY, C, BF))
            if t > half:
                outs.append(shape(dm.rows_of(n - 1 - t), C, BF))
            scratch = conv_scratch(dm, dm.rows_of(t), dm.rows_of(t - 1))
        results = call(
            functools.partial(backward_kernel, dm, t, has_skip),
            [me], operands, outs, scratch,
            2 * dm.rows_of(max(t - 1, 0)) * 28 * C * C if t > 0 else 1000,
        )
        block = results[0]
        if t > 0:
            down = hop(results[1], t, t - 1)
            if t > half:
                skip_grads[n - 1 - t] = hop(results[2], t, n - 1 - t)

    held[0], _ = lax.optimization_barrier((held[0], block))
    xt, bt = call(
        functools.partial(turn_kernel, dm),
        [me], held + branches,
        [shape(9 * C, cells_all, BF), shape(C, cells_all, BF)],
        [pltpu.VMEM((cells_all + 2 * PAD, C), F32)],
        2 * 10 * cells_all * C * 100,
    )
    near = [block] + [rotate(block, r) for r in range(1, parts)]
    *far, xt = lax.optimization_barrier((*near[1:], xt))
    near = [block] + far
    blocks = list(near)
    for e in range(1, micro):
        blocks += [swap(b, e) for b in near]
    operands = [xt, bt, *blocks]
    scratch = [
        pltpu.VMEM((micro * (W + 2) * G, C), BF),
        pltpu.VMEM((27, C, C), F32),
        pltpu.VMEM((slabs, 8, C), F32),
        pltpu.SemaphoreType.DMA((27,)),
    ]
    outs = [
        jax.ShapeDtypeStruct((9, 3, C, C), F32),
        shape(C, C, F32),
        shape(dm.offs, C, F32),
        shape(1, 1, F32),
    ]
    moved = nbytes(operands) + nbytes(outs)
    grad, mix, heads, loss = pl.pallas_call(
        functools.partial(weight_kernel, dm),
        name="weights",
        out_shape=outs,
        in_specs=[scalar()] + [whole()] * len(operands),
        out_specs=[pl.BlockSpec(memory_space=pl.ANY), whole(), whole(), whole()],
        scratch_shapes=scratch,
        compiler_params=pltpu.CompilerParams(
            vmem_limit_bytes=nbytes(operands) + nbytes(scratch[:3]) + SPARE
        ),
        cost_estimate=pl.CostEstimate(
            flops=2 * cells_all * 28 * C * C, bytes_accessed=moved, transcendentals=0
        ),
    )(me, *operands)
    return (
        loss[0, 0],
        grad.reshape((1, 3, 3, 3, C, C)),
        mix[None],
        jnp.transpose(heads),
    )


def solution(mesh):
    placed = (
        P(None, None, "slab", None, None),
        P(None, "slab", None, None),
        P(),
        P("section", None, None, None, None, None),
        P("section", None, None),
        P(),
    )
    return jax.shard_map(
        body,
        mesh=mesh,
        in_specs=placed,
        out_specs=(P(), P("section", None, None, None, None, None), P("section", None, None), P()),
        check_vma=False,
    )
```

```python
import functools
import math

import jax
import jax.numpy as jnp
from jax import lax
from jax.experimental import pallas as pl
from jax.experimental.pallas import tpu as pltpu
from jax.sharding import PartitionSpec as P


loss_scale = 1024.0
BF = jnp.bfloat16
F32 = jnp.float32
PAD = 8
SPARE = 6 * 1024 * 1024
CARRY = 16


class Dims:
    def __init__(self, sections, slabs, micro, channels, depth, rows, cols, offs):
        self.sections, self.half = sections, sections // 2
        self.slabs, self.micro = slabs, micro
        self.C, self.D, self.R, self.W, self.offs = channels, depth, rows, cols, offs
        self.G = depth * rows
        self.parts = slabs // micro
        self.own = cols // self.parts
        self.count = micro * offs * depth * rows * cols

    def fwd(self, t):
        return 2 * (self.sections - 1) - t

    def rows_of(self, k):
        return (self.own + 2 * k) * self.G


def group_mask(dm, kz, ky):
    g = lax.broadcasted_iota(jnp.int32, (1, dm.G, dm.C), 1)
    d = g // dm.R + kz
    r = g % dm.R + ky
    return (d >= 0) & (d < dm.D) & (r >= 0) & (r < dm.R)


def column_mask(dm, base, k, width):
    col = lax.broadcasted_iota(jnp.int32, (width, dm.G, dm.C), 0) + (base - k)
    return (col >= 0) & (col < dm.W)


def spread(dm, xf, x27, width, sign):
    G, C = dm.G, dm.C
    rin = (width + 2) * G
    for kz in range(3):
        for ky in range(3):
            dz, dy = sign * (kz - 1), sign * (ky - 1)
            delta = dz * dm.R + dy
            part = xf[PAD + delta:PAD + delta + rin, :]
            if kz != 1 or ky != 1:
                part = part.reshape(width + 2, G, C)
                part = jnp.where(group_mask(dm, dz, dy), part, 0.0).reshape(rin, C)
            part = part.astype(BF)
            for kx in range(3):
                first = (1 + sign * (kx - 1)) * G
                tap = (kz * 3 + ky) * 3 + kx
                x27[0:width * G, tap * C:(tap + 1) * C] = part[first:first + width * G]


def dot(a, b):
    return lax.dot_general(a, b, (((1,), (0,)), ((), ())), preferred_element_type=F32)


def dot_nt(a, b):
    return lax.dot_general(a, b, (((1,), (1,)), ((), ())), preferred_element_type=F32)


def dot_tn(a, b):
    return lax.dot_general(a, b, (((0,), (0,)), ((), ())), preferred_element_type=F32)


def stage(xf, x, rin):
    xf[PAD:PAD + rin, :] = x.astype(F32)


def preact(dm, t, xf, x27, skip_ref, w_ref, b_ref):
    width = dm.own + 2 * dm.fwd(t)
    ro = width * dm.G
    spread(dm, xf, x27, width, 1)
    if t <= dm.half:
        branch = x27[0:ro, 13 * dm.C:14 * dm.C]
    else:
        branch = skip_ref[0:ro, :]
    return dot(x27[0:ro, :], w_ref[...]) + dot(branch, b_ref[...])


def silu_masked(dm, base, k, pre):
    width = dm.own + 2 * k
    value = pre * (1.0 / (1.0 + jnp.exp(-pre)))
    value = value.reshape(width, dm.G, dm.C)
    value = jnp.where(column_mask(dm, base, k, width), value, 0.0)
    return value.reshape(width * dm.G, dm.C).astype(BF)


def pre_gradient(dm, base, k, upstream, pre):
    width = dm.own + 2 * k
    sig = 1.0 / (1.0 + jnp.exp(-pre))
    value = upstream * (sig * (1.0 + pre * (1.0 - sig)))
    value = value.reshape(width, dm.G, dm.C)
    value = jnp.where(column_mask(dm, base, k, width), value, 0.0)
    return value.reshape(width * dm.G, dm.C).astype(BF)


def forward_kernel(dm, t, has_skip_in, has_mirror, *refs):
    refs = list(refs)
    count = dm.parts if t == 0 else 1
    me_ref, x_refs = refs[0], refs[1:1 + count]
    w_ref, b_ref = refs[1 + count:3 + count]
    at = 3 + count
    x_ref = x_refs[0]
    skip_ref = kept_ref = None
    if has_skip_in:
        skip_ref = refs[at]
        at += 1
    if t > 0:
        kept_ref = refs[at]
        at += 1
    y_ref, pre_ref, own_ref = refs[at:at + 3]
    at += 3
    if has_mirror:
        mirror_ref = refs[at]
        at += 1
    if t == 0:
        lab_ref, xg = refs[at], refs[-1]
        at += 1
        wide = dm.own + 2 * (dm.fwd(0) + 1)
        layers = dm.G // dm.parts
        for r in range(dm.parts):
            place = lax.rem(me_ref[0] + (dm.parts - r), dm.parts)
            xg[pl.ds(place * layers, layers)] = x_refs[r][...].astype(F32)
        lab_ref[...] = xg[:, wide, :]
    xf, x27 = refs[at:at + 2]

    @pl.when(me_ref[2] == t)
    def _():
        base = me_ref[0] * dm.own
        k = dm.fwd(t)
        if t == 0:
            gather_cells(dm, xg, xf)
        else:
            stage(xf, x_ref[...], dm.rows_of(k + 1))
        size, mid = dm.own * dm.G, (k + 1) * dm.G
        own_ref[...] = xf[PAD + mid:PAD + mid + size, :].astype(BF)
        pre = preact(dm, t, xf, x27, skip_ref, w_ref, b_ref)
        first = (k - t) * dm.G
        pre_ref[...] = pre[first:first + dm.rows_of(t)]
        y = silu_masked(dm, base, k, pre)
        y_ref[...] = y
        if has_mirror:
            keep = dm.fwd(dm.sections - 1 - t)
            first = (k - keep) * dm.G
            mirror_ref[...] = y[first:first + dm.rows_of(keep)]

    if t > 0:
        @pl.when(me_ref[2] != t)
        def _():
            own_ref[...] = kept_ref[...]


def split_kernel(dm, me_ref, f_ref, l_ref, *refs):
    outs, marks = refs[:dm.micro], refs[dm.micro]
    W = dm.W
    layers = f_ref.shape[0] // dm.micro
    for e in range(dm.micro):
        crop = lax.rem(me_ref[1] + e, dm.micro)
        marks[...] = jnp.zeros(marks.shape, F32)
        for layer in range(layers):
            at = crop * layers + layer
            outs[e][layer * W:(layer + 1) * W, :] = f_ref[at]
            marks[layer:layer + 1, 0:W] = l_ref[at].astype(F32)
        outs[e][layers * W:, :] = marks[...].astype(BF)


def window_kernel(dm, wing, cols, me_ref, *refs):
    crops, outs, xs = refs[:dm.micro], refs[dm.micro:-1], refs[-1]
    C, W, own = dm.C, dm.W, dm.own
    layers = dm.G // dm.slabs
    xs[0:16, :] = jnp.zeros((16, C), F32)
    xs[wing + W:, :] = jnp.zeros((xs.shape[0] - wing - W, C), F32)
    row = lax.broadcasted_iota(jnp.int32, (cols, C), 0)
    for e in range(dm.micro):
        crop = crops[e][...].astype(F32)
        core = lax.rem(me_ref[1] + (dm.micro - e), dm.micro)
        for layer in range(layers):
            xs[wing:wing + W, :] = crop[layer * W:(layer + 1) * W]
            mark = crop[layers * W + layer:layers * W + layer + 1]
            for r in range(dm.parts):
                place = lax.rem(me_ref[0] + r, dm.parts)
                start = pl.multiple_of(place * own, 8)
                value = jnp.where(row == own + 2 * wing, mark, xs[pl.ds(start, cols), :])
                outs[r][core * layers + layer] = value.astype(BF)


def gather_cells(dm, xg, xf):
    rows = (dm.own + 2 * (dm.fwd(0) + 1)) * dm.G
    cells = jnp.transpose(xg[...], (1, 0, 2))
    cells = cells.reshape(cells.shape[0] * dm.G, dm.C)
    xf[PAD:PAD + rows, :] = cells[0:rows]


def load_kernel(chunks, w_ref, b_ref, out_ref, out_b_ref, sems):
    rows = w_ref.shape[0] // chunks
    copies = []
    for i in range(chunks):
        part = pl.ds(i * rows, rows)
        copies.append(pltpu.make_async_copy(w_ref.at[part], out_ref.at[part], sems.at[i]))
        copies[i].start()
    copies.append(pltpu.make_async_copy(b_ref, out_b_ref, sems.at[chunks]))
    copies[chunks].start()
    for copy in copies:
        copy.wait()


def stack_kernel(*refs):
    rows = refs[0].shape[0]
    for i, ref in enumerate(refs[:-1]):
        refs[-1][i * rows:(i + 1) * rows, :] = ref[...]


def flip_kernel(C, w_ref, out_ref):
    for tap in range(27):
        out_ref[tap * C:(tap + 1) * C, :] = jnp.transpose(w_ref[tap * C:(tap + 1) * C, :])


def back_conv(dm, t, pg, xf, x27, wt_ref, b_ref, msg_ref):
    width = dm.own + 2 * (t - 1)
    stage(xf, pg, dm.rows_of(t))
    spread(dm, xf, x27, width, -1)
    grad = dot(x27[0:width * dm.G, :], wt_ref[...])
    if t <= dm.half:
        grad = grad + dot_nt(pg[dm.G:dm.G + width * dm.G], b_ref[...])
    msg_ref[0:width * dm.G, :] = grad.astype(BF)


def flat_labels(dm, base, width, lab_ref):
    G, cells = dm.G, width * dm.G
    lanes = dm.C
    cell = lax.broadcasted_iota(jnp.int32, (lanes, cells), 1)
    row = lax.broadcasted_iota(jnp.int32, (lanes, cells), 0)
    pick = jnp.where((cell // G + base == row) & (row < dm.W), 1.0, 0.0).astype(BF)
    found = dot(lab_ref[...].astype(BF), pick)
    g = lax.broadcasted_iota(jnp.int32, (G, cells), 1) % G
    row = lax.broadcasted_iota(jnp.int32, (G, cells), 0)
    line = jnp.sum(jnp.where(g == row, found, 0.0), axis=0, keepdims=True)
    return jnp.broadcast_to(line, (8, cells))


def affinity(dm, width, lab, off_ref):
    G, cells = dm.G, width * dm.G
    total = lab.shape[1]
    mid = lab[:, G:G + cells]
    row = lax.broadcasted_iota(jnp.int32, (8, cells), 0)
    g = lax.broadcasted_iota(jnp.int32, (8, cells), 1) % G
    d, r = g // dm.R, g % dm.R
    target = jnp.zeros((8, cells), F32)
    for j in range(dm.offs):
        dz, dy, dx = off_ref[j, 0], off_ref[j, 1], off_ref[j, 2]
        shift = G + dx * G + dz * dm.R + dy
        near = pltpu.roll(lab, lax.rem(2 * total - shift, total), 1)[:, 0:cells]
        inside = (d + dz >= 0) & (d + dz < dm.D) & (r + dy >= 0) & (r + dy < dm.R)
        same = inside & (near == mid) & (mid != 0.0) & (row == j)
        target = jnp.where(same, 1.0, target)
    return target


def target_kernel(dm, me_ref, off_ref, lab_ref, out_ref):
    t = dm.sections - 1
    lab = flat_labels(dm, me_ref[0] * dm.own - t - 1, dm.own + 2 * t + 2, lab_ref)
    out_ref[...] = affinity(dm, dm.own + 2 * t, lab, off_ref)


def last_kernel(dm, *refs):
    (me_ref, x_ref, w_ref, b_ref, skip_ref, kept_ref, wt_ref, head_ref, target_ref) = refs[:9]
    msg_ref, pgx_ref, skip_out, own_ref, xf, x27, lines = refs[9:]
    t = dm.sections - 1

    @pl.when(me_ref[2] == t)
    def _():
        base = me_ref[0] * dm.own
        G, C, own = dm.G, dm.C, dm.own
        mid, size = t * G, own * G
        own_ref[...] = x_ref[mid + G:mid + G + size, :]
        stage(xf, x_ref[...], dm.rows_of(t + 1))
        pre = preact(dm, t, xf, x27, skip_ref, w_ref, b_ref)
        y = silu_masked(dm, base, t, pre)
        logits = dot_nt(head_ref[...], y)
        target = target_ref[...]
        live = lax.broadcasted_iota(jnp.int32, logits.shape, 0) < dm.offs
        sig = 1.0 / (1.0 + jnp.exp(-logits))
        lg = jnp.where(live, loss_scale * (sig - target) / dm.count, 0.0).astype(BF)
        term = jnp.maximum(logits, 0.0) + jnp.log(1.0 + jnp.exp(-jnp.abs(logits))) - target * logits
        term = jnp.where(live, term, 0.0)[:, mid:mid + size]
        loss = jnp.sum(jnp.sum(term, axis=1, keepdims=True), axis=0, keepdims=True)
        head_part = dot(lg[:, mid:mid + size], y[mid:mid + size])
        used = dm.offs + 1
        lines[...] = jnp.zeros(lines.shape, F32)
        lines[0:dm.offs, :] = head_part[0:dm.offs]
        lines[dm.offs:used, :] = jnp.broadcast_to(loss, (1, C))
        rest = lines[0:8, :]
        for i in range(3):
            piece = rest.astype(BF).astype(F32)
            lines[i * used:(i + 1) * used, :] = piece[0:used]
            rest = rest - piece
        carry = lines[...].astype(BF)
        upstream = dot_tn(lg, head_ref[...])
        pg = pre_gradient(dm, base, t, upstream, pre)
        pgx_ref[0:size, :] = pg[mid:mid + size]
        pgx_ref[size:size + CARRY, :] = carry
        back_conv(dm, t, pg, xf, x27, wt_ref, b_ref, msg_ref)
        end = dm.rows_of(t - 1)
        msg_ref[end:end + CARRY, :] = carry
        m = dm.sections - 1 - t
        first = (t - m) * G
        skip_out[...] = dot_nt(pg[first:first + dm.rows_of(m)], b_ref[...]).astype(BF)

    @pl.when(me_ref[2] != t)
    def _():
        own_ref[...] = kept_ref[...]


def backward_kernel(dm, t, has_skip_in, *refs):
    refs = list(refs)
    me_ref, down_ref, pre_ref, kept_ref = refs[:4]
    at = 4
    if t > 0:
        wt_ref, b_ref = refs[at:at + 2]
        at += 2
    if has_skip_in:
        skip_ref = refs[at]
        at += 1
    pgx_ref = refs[at]
    at += 1
    if t > 0:
        msg_ref = refs[at]
        at += 1
        if t > dm.half:
            skip_out = refs[at]
            at += 1
        xf, x27 = refs[at:at + 2]

    @pl.when(me_ref[2] == t)
    def _():
        base = me_ref[0] * dm.own
        ro = dm.rows_of(t)
        upstream = down_ref[0:ro, :].astype(F32)
        if has_skip_in:
            upstream = upstream + skip_ref[0:ro, :].astype(F32)
        pg = pre_gradient(dm, base, t, upstream, pre_ref[...])
        mid, size = t * dm.G, dm.own * dm.G
        carry = down_ref[ro:ro + CARRY, :]
        pgx_ref[0:size, :] = pg[mid:mid + size]
        pgx_ref[size:size + CARRY, :] = carry
        if t > 0:
            back_conv(dm, t, pg, xf, x27, wt_ref, b_ref, msg_ref)
            end = dm.rows_of(t - 1)
            msg_ref[end:end + CARRY, :] = carry
            if t > dm.half:
                m = dm.sections - 1 - t
                first = (t - m) * dm.G
                skip_out[...] = dot_nt(pg[first:first + dm.rows_of(m)], b_ref[...]).astype(BF)

    @pl.when(me_ref[2] != t)
    def _():
        pgx_ref[...] = kept_ref[...]


def turn_kernel(dm, *refs):
    q_ref = refs[0]
    x_refs = refs[1:1 + dm.slabs]
    b_refs = refs[1 + dm.slabs:1 + dm.slabs + dm.micro]
    xt_ref, bt_ref, xf = refs[1 + dm.slabs + dm.micro:]
    C, size = dm.C, dm.own * dm.G
    cells = dm.slabs * size
    for e in range(dm.micro):
        for r in range(dm.parts):
            block = e * dm.parts + r
            place = lax.rem(q_ref[0] + (dm.parts - r), dm.parts) + e * dm.parts
            at = pl.multiple_of(place * size, size)
            xf[pl.ds(PAD + at, size), :] = x_refs[block][...].astype(F32)

            @pl.when(q_ref[2] > dm.half)
            def _():
                bt_ref[:, pl.ds(at, size)] = jnp.transpose(b_refs[e][r * size:(r + 1) * size, :])

    for kz in range(3):
        for ky in range(3):
            delta = (kz - 1) * dm.R + ky - 1
            part = xf[PAD + delta:PAD + delta + cells, :]
            if kz != 1 or ky != 1:
                part = part.reshape(cells // dm.G, dm.G, C)
                part = jnp.where(group_mask(dm, kz - 1, ky - 1), part, 0.0).reshape(cells, C)
            tap = kz * 3 + ky
            xt_ref[tap * C:(tap + 1) * C, :] = jnp.transpose(part.astype(BF))


def weight_kernel(dm, *refs):
    q_ref, xt_ref, bt_ref = refs[:3]
    ahead, behind = refs[3:3 + dm.slabs], refs[3 + dm.slabs:3 + 2 * dm.slabs]
    grad_ref, mix_ref, head_ref, loss_ref, full, held, sums, sems = refs[3 + 2 * dm.slabs:]
    G, C, W = dm.G, dm.C, dm.W
    size = dm.own * G
    span = (W + 2) * G
    cells = W * G
    for e in range(dm.micro):
        start = e * span
        full[start:start + G, :] = jnp.zeros((G, C), BF)
        full[start + (W + 1) * G:start + span, :] = jnp.zeros((G, C), BF)

    def place_blocks(blocks):
        for e in range(dm.micro):
            for r in range(dm.parts):
                block = blocks[e * dm.parts + r]
                place = lax.rem(q_ref[0] + (dm.parts - r), dm.parts)
                at = pl.multiple_of(e * span + G + place * size, 16)
                full[pl.ds(at, size), :] = block[0:size, :]
                carry = block[size:size + CARRY, :].astype(F32)
                slot = lax.rem(q_ref[1] + (dm.micro - e), dm.micro) * dm.parts + place
                used = dm.offs + 1
                sums[slot, 0:used] = (carry[0:used] + carry[used:2 * used]) + carry[2 * used:3 * used]

    @pl.when(q_ref[2] == 0)
    def _():
        place_blocks(behind)

    @pl.when(q_ref[2] != 0)
    def _():
        place_blocks(ahead)

    def product(lhs_ref, row, count, kx):
        total = None
        for e in range(dm.micro):
            first = e * span + (2 - kx) * G
            one = dot(lhs_ref[row:row + count, e * cells:(e + 1) * cells], full[first:first + cells, :])
            total = one if total is None else total + one
        return total

    copies = []
    for step in range(27):
        kx, tap = step // 9, step % 9
        held[step] = product(xt_ref, tap * C, C, kx)
        copies.append(pltpu.make_async_copy(held.at[step], grad_ref.at[tap, kx], sems.at[step]))
        copies[step].start()

    @pl.when(q_ref[2] > dm.half)
    def _():
        mix_ref[...] = product(bt_ref, 0, C, 1)

    @pl.when(q_ref[2] <= dm.half)
    def _():
        mix_ref[...] = held[13]

    total = jnp.zeros((8, C), F32)
    for slot in range(dm.slabs):
        total = total + sums[slot]
    head_ref[...] = total[0:dm.offs]
    loss_ref[...] = total[dm.offs:dm.offs + 1, 0:1] / dm.count
    for copy in copies:
        copy.wait()


def whole():
    return pl.BlockSpec(memory_space=pltpu.VMEM)


def scalar():
    return pl.BlockSpec(memory_space=pltpu.SMEM)


def shape(rows, cols, kind):
    return jax.ShapeDtypeStruct((rows, cols), kind)


def nbytes(arrays):
    return sum(math.prod(a.shape) * jnp.dtype(a.dtype).itemsize for a in arrays)


def call(kernel, scalars, operands, outs, scratch, flops, places=None):
    moved = nbytes(operands) + nbytes(outs)
    room = moved + nbytes([a for a in scratch if a.dtype in (BF, F32)]) + SPARE
    return pl.pallas_call(
        kernel,
        out_shape=outs,
        in_specs=[scalar()] * len(scalars) + [whole()] * len(operands),
        out_specs=places or [whole()] * len(outs),
        scratch_shapes=scratch,
        compiler_params=pltpu.CompilerParams(vmem_limit_bytes=room),
        cost_estimate=pl.CostEstimate(flops=flops, bytes_accessed=moved, transcendentals=0),
    )(*scalars, *operands)


def conv_scratch(dm, rin, ro):
    return [
        pltpu.VMEM((rin + 2 * PAD, dm.C), F32),
        pltpu.VMEM((ro, 27 * dm.C), BF),
    ]


def body(features_in, labels, offsets, conv_weight, branch_weight, head_weight):
    n = lax.axis_size("section")
    slabs = lax.axis_size("slab")
    micro, C, thick, R, W = features_in.shape
    dm = Dims(n, slabs, micro, C, thick * slabs, R, W, offsets.shape[0])
    G, own, parts, half = dm.G, dm.own, dm.parts, dm.half
    section = lax.axis_index("section")
    slab = lax.axis_index("slab")
    c, q = lax.rem(slab, micro), lax.div(slab, micro)
    me = jnp.stack([q, c, section]).astype(jnp.int32)
    size = own * G

    def hop(x, source, target):
        return lax.ppermute(x, "section", [(source, target)])

    def rotate(x, r):
        pairs = [(p * micro + e, ((p + r) % parts) * micro + e) for p in range(parts) for e in range(micro)]
        return lax.ppermute(x, "slab", pairs)

    def swap(x, e):
        pairs = [(p * micro + i, p * micro + (i + e) % micro) for p in range(parts) for i in range(micro)]
        return lax.ppermute(x, "slab", pairs)

    def along(x, pairs, first, last):
        joint = [(s * slabs + i, s * slabs + j) for s in range(first, last) for i, j in pairs]
        return lax.ppermute(x, ("section", "slab"), joint)

    def turns(block, first, last):
        found = [block]
        for r in range(1, parts):
            pairs = [(p * micro + e, (p + r) % parts * micro + e) for p in range(parts) for e in range(micro)]
            found.append(along(block, pairs, first, last))
        return found

    def swaps(blocks, first, last):
        found = list(blocks)
        for e in range(1, micro):
            pairs = [(p * micro + i, p * micro + (i + e) % micro) for p in range(parts) for i in range(micro)]
            found += [along(b, pairs, first, last) for b in blocks]
        return found

    source = conv_weight[0].reshape(27 * C, C)
    held_hbm = pl.BlockSpec(memory_space=pltpu.HBM)
    kernel, mixing = pl.pallas_call(
        functools.partial(load_kernel, 9),
        name="load",
        out_shape=[shape(27 * C, C, BF), shape(C, C, BF)],
        in_specs=[held_hbm, held_hbm],
        out_specs=[whole(), whole()],
        scratch_shapes=[pltpu.SemaphoreType.DMA((10,))],
        compiler_params=pltpu.CompilerParams(vmem_limit_bytes=27 * C * C * 2 + SPARE),
        cost_estimate=pl.CostEstimate(flops=0, bytes_accessed=27 * C * C * 4, transcendentals=0),
    )(source, branch_weight[0])

    wing = dm.fwd(0) + 1
    wide = own + 2 * wing
    cols = -(-(wide + 1) // 16) * 16
    layers = thick * R
    cells = jnp.transpose(features_in, (0, 2, 3, 4, 1)).reshape(micro * layers, W, C)
    lines = -(-layers // 16) * 16
    crops = list(call(
        functools.partial(split_kernel, dm),
        [me], [cells, labels.reshape(micro * layers, 1, W)],
        [shape(layers * W + lines, C, BF)] * micro,
        [pltpu.VMEM((lines, C), F32)],
        1000,
    ))
    for e in range(1, micro):
        crops[e] = swap(crops[e], e)
    windows = call(
        functools.partial(window_kernel, dm, wing, cols),
        [me], crops,
        [jax.ShapeDtypeStruct((micro * layers, cols, C), BF)] * parts,
        [pltpu.VMEM((-(-(wing + W + cols) // 8) * 8, C), F32)],
        1000,
    )
    current = [windows[0]]
    for r in range(1, parts):
        current.append(rotate(windows[r], r))

    head = jnp.pad(jnp.transpose(head_weight), ((0, 8 - dm.offs), (0, 0)))

    pres, mirrors = [], {}
    kept = kernel_t = None
    for t in range(n - 1):
        k = dm.fwd(t)
        has_skip, has_mirror = t > half, t < half - 1
        operands = [*(current if t == 0 else [current]), kernel, mixing]
        if has_skip:
            operands.append(mirrors[t])
        if t > 0:
            operands.append(kept)
        outs = [shape(dm.rows_of(k), C, BF), shape(dm.rows_of(t), C, F32), shape(size, C, BF)]
        scratch = conv_scratch(dm, dm.rows_of(k + 1), dm.rows_of(k))
        if has_mirror:
            outs.append(shape(dm.rows_of(dm.fwd(n - 1 - t)), C, BF))
        if t == 0:
            outs.append(shape(G, C, F32))
            scratch.append(pltpu.VMEM((G, cols, C), F32))
        results = call(
            functools.partial(forward_kernel, dm, t, has_skip, has_mirror),
            [me], operands, outs, scratch,
            2 * dm.rows_of(k) * 28 * C * C,
        )
        pres.append(results[1])
        kept = results[2]
        current = hop(results[0], t, t + 1)
        if t == 0:
            marks = results[-1]
            raw, marks, _ = lax.optimization_barrier((kernel, marks, results[0]))
            targets = call(
                functools.partial(target_kernel, dm), [me, offsets], [marks],
                [shape(8, dm.rows_of(n - 1), F32)], [], 1000,
            )[0]
            kernel_t = call(
                functools.partial(flip_kernel, C), [], [raw],
                [shape(27 * C, C, BF)], [], 2 * 27 * C * C * 100,
            )[0]
        if has_mirror:
            later, current = lax.optimization_barrier((results[3], current))
            mirrors[n - 1 - t] = hop(later, t, n - 1 - t)

    t = n - 1
    skip = mirrors[t]
    branch = skip[t * G:t * G + size]
    for s in range(half + 1, n - 1):
        first = dm.fwd(s) * G
        branch = jnp.where(section == s, mirrors[s][first:first + size], branch)
    branch, _ = lax.optimization_barrier((branch, results[0]))
    branches = call(
        stack_kernel, [], turns(branch, half + 1, n),
        [shape(parts * size, C, BF)], [], 1000,
    )
    branches = swaps(branches, half + 1, n)
    outs = [
        shape(dm.rows_of(t - 1) + CARRY, C, BF),
        shape(size + CARRY, C, BF),
        shape(dm.rows_of(0), C, BF),
        shape(size, C, BF),
    ]
    results = call(
        functools.partial(last_kernel, dm),
        [me],
        [current, kernel, mixing, skip, kept, kernel_t, head, targets],
        outs,
        conv_scratch(dm, dm.rows_of(t + 1), dm.rows_of(t)) + [pltpu.VMEM((CARRY, C), F32)],
        4 * dm.rows_of(t) * 28 * C * C,
    )
    down = hop(results[0], t, t - 1)
    block, held = results[1], results[3]
    skip_grads = {0: hop(results[2], t, 0)}
    held = swaps(turns(held, 0, n), 0, n)
    cells_all = micro * W * G

    for t in range(n - 2, -1, -1):
        has_skip = t < half - 1
        operands = [down, pres[t], block]
        if t > 0:
            operands += [kernel_t, mixing]
        if has_skip:
            operands.append(skip_grads[t])
        outs = [shape(size + CARRY, C, BF)]
        scratch = []
        if t > 0:
            outs.append(shape(dm.rows_of(t - 1) + CARRY, C, BF))
            if t > half:
                outs.append(shape(dm.rows_of(n - 1 - t), C, BF))
            scratch = conv_scratch(dm, dm.rows_of(t), dm.rows_of(t - 1))
        results = call(
            functools.partial(backward_kernel, dm, t, has_skip),
            [me], operands, outs, scratch,
            2 * dm.rows_of(max(t - 1, 0)) * 28 * C * C if t > 0 else 1000,
        )
        block = results[0]
        if t == 1:
            later = block
        if t > 0:
            down = hop(results[1], t, t - 1)
            if t > half:
                skip_grads[n - 1 - t] = hop(results[2], t, n - 1 - t)

    held[0], _ = lax.optimization_barrier((held[0], block))
    xt, bt = call(
        functools.partial(turn_kernel, dm),
        [me], held + branches,
        [shape(9 * C, cells_all, BF), shape(C, cells_all, BF)],
        [pltpu.VMEM((cells_all + 2 * PAD, C), F32)],
        2 * 10 * cells_all * C * 100,
    )
    ahead = turns(later, 1, n)
    behind = turns(block, 0, 1)
    *far, xt = lax.optimization_barrier((*ahead[1:], *behind[1:], xt))
    ahead = swaps([later] + far[:parts - 1], 1, n)
    behind = swaps([block] + far[parts - 1:], 0, 1)
    blocks = ahead + behind
    operands = [xt, bt, *blocks]
    scratch = [
        pltpu.VMEM((micro * (W + 2) * G, C), BF),
        pltpu.VMEM((27, C, C), F32),
        pltpu.VMEM((slabs, 8, C), F32),
        pltpu.SemaphoreType.DMA((27,)),
    ]
    outs = [
        jax.ShapeDtypeStruct((9, 3, C, C), F32),
        shape(C, C, F32),
        shape(dm.offs, C, F32),
        shape(1, 1, F32),
    ]
    moved = nbytes(operands) + nbytes(outs)
    grad, mix, heads, loss = pl.pallas_call(
        functools.partial(weight_kernel, dm),
        name="weights",
        out_shape=outs,
        in_specs=[scalar()] + [whole()] * len(operands),
        out_specs=[pl.BlockSpec(memory_space=pl.ANY), whole(), whole(), whole()],
        scratch_shapes=scratch,
        compiler_params=pltpu.CompilerParams(
            vmem_limit_bytes=nbytes(operands) + nbytes(scratch[:3]) + SPARE
        ),
        cost_estimate=pl.CostEstimate(
            flops=2 * cells_all * 28 * C * C, bytes_accessed=moved, transcendentals=0
        ),
    )(me, *operands)
    return (
        loss[0, 0],
        grad.reshape((1, 3, 3, 3, C, C)),
        mix[None],
        jnp.transpose(heads),
    )


def solution(mesh):
    placed = (
        P(None, None, "slab", None, None),
        P(None, "slab", None, None),
        P(),
        P("section", None, None, None, None, None),
        P("section", None, None),
        P(),
    )
    return jax.shard_map(
        body,
        mesh=mesh,
        in_specs=placed,
        out_specs=(P(), P("section", None, None, None, None, None), P("section", None, None), P()),
        check_vma=False,
    )
```

```python
import functools
import math

import jax
import jax.numpy as jnp
from jax import lax
from jax.experimental import pallas as pl
from jax.experimental.pallas import tpu as pltpu
from jax.sharding import PartitionSpec as P


loss_scale = 1024.0
BF = jnp.bfloat16
F32 = jnp.float32
PAD = 8
SPARE = 6 * 1024 * 1024
CARRY = 16


class Dims:
    def __init__(self, sections, slabs, micro, channels, depth, rows, cols, offs):
        self.sections, self.half = sections, sections // 2
        self.slabs, self.micro = slabs, micro
        self.C, self.D, self.R, self.W, self.offs = channels, depth, rows, cols, offs
        self.G = depth * rows
        self.parts = slabs // micro
        self.own = cols // self.parts
        self.count = micro * offs * depth * rows * cols

    def fwd(self, t):
        return 2 * (self.sections - 1) - t

    def rows_of(self, k):
        return (self.own + 2 * k) * self.G


def group_mask(dm, kz, ky):
    g = lax.broadcasted_iota(jnp.int32, (1, dm.G, dm.C), 1)
    d = g // dm.R + kz
    r = g % dm.R + ky
    return (d >= 0) & (d < dm.D) & (r >= 0) & (r < dm.R)


def column_mask(dm, base, k, width):
    col = lax.broadcasted_iota(jnp.int32, (width, dm.G, dm.C), 0) + (base - k)
    return (col >= 0) & (col < dm.W)


def spread(dm, xf, x27, width, sign):
    G, C = dm.G, dm.C
    rin = (width + 2) * G
    for kz in range(3):
        for ky in range(3):
            dz, dy = sign * (kz - 1), sign * (ky - 1)
            delta = dz * dm.R + dy
            part = xf[PAD + delta:PAD + delta + rin, :]
            if kz != 1 or ky != 1:
                part = part.reshape(width + 2, G, C)
                part = jnp.where(group_mask(dm, dz, dy), part, 0.0).reshape(rin, C)
            part = part.astype(BF)
            for kx in range(3):
                first = (1 + sign * (kx - 1)) * G
                tap = (kz * 3 + ky) * 3 + kx
                x27[0:width * G, tap * C:(tap + 1) * C] = part[first:first + width * G]


def dot(a, b):
    return lax.dot_general(a, b, (((1,), (0,)), ((), ())), preferred_element_type=F32)


def dot_nt(a, b):
    return lax.dot_general(a, b, (((1,), (1,)), ((), ())), preferred_element_type=F32)


def dot_tn(a, b):
    return lax.dot_general(a, b, (((0,), (0,)), ((), ())), preferred_element_type=F32)


def stage(xf, x, rin):
    xf[PAD:PAD + rin, :] = x.astype(F32)


def preact(dm, t, xf, x27, skip_ref, w_ref, b_ref):
    width = dm.own + 2 * dm.fwd(t)
    ro = width * dm.G
    spread(dm, xf, x27, width, 1)
    if t <= dm.half:
        branch = x27[0:ro, 13 * dm.C:14 * dm.C]
    else:
        branch = skip_ref[0:ro, :]
    return dot(x27[0:ro, :], w_ref[...]) + dot(branch, b_ref[...])


def logistic(value):
    return 1.0 / (1.0 + jnp.exp(-value))


def inside(dm, base, k, value):
    width = dm.own + 2 * k
    value = value.reshape(width, dm.G, dm.C)
    value = jnp.where(column_mask(dm, base, k, width), value, 0.0)
    return value.reshape(width * dm.G, dm.C).astype(BF)


def silu_masked(dm, base, k, pre, sig):
    return inside(dm, base, k, pre * sig)


def pre_gradient(dm, base, k, upstream, pre, sig):
    return inside(dm, base, k, upstream * (sig * (1.0 + pre * (1.0 - sig))))


def forward_kernel(dm, t, has_skip_in, has_mirror, *refs):
    refs = list(refs)
    count = dm.parts if t == 0 else 1
    me_ref, x_refs = refs[0], refs[1:1 + count]
    w_ref, b_ref = refs[1 + count:3 + count]
    at = 3 + count
    x_ref = x_refs[0]
    skip_ref = kept_ref = None
    if has_skip_in:
        skip_ref = refs[at]
        at += 1
    if t > 0:
        kept_ref = refs[at]
        at += 1
    y_ref, pre_ref, own_ref = refs[at:at + 3]
    at += 3
    if has_mirror:
        mirror_ref = refs[at]
        at += 1
    if t == 0:
        lab_ref, xg = refs[at], refs[-1]
        at += 1
        wide = dm.own + 2 * (dm.fwd(0) + 1)
        layers = dm.G // dm.parts
        for r in range(dm.parts):
            place = lax.rem(me_ref[0] + (dm.parts - r), dm.parts)
            xg[pl.ds(place * layers, layers)] = x_refs[r][...].astype(F32)
        lab_ref[...] = xg[:, wide, :]
    xf, x27 = refs[at:at + 2]

    @pl.when(me_ref[2] == t)
    def _():
        base = me_ref[0] * dm.own
        k = dm.fwd(t)
        if t == 0:
            gather_cells(dm, xg, xf)
        else:
            stage(xf, x_ref[...], dm.rows_of(k + 1))
        size, mid = dm.own * dm.G, (k + 1) * dm.G
        own_ref[...] = xf[PAD + mid:PAD + mid + size, :].astype(BF)
        pre = preact(dm, t, xf, x27, skip_ref, w_ref, b_ref)
        first = (k - t) * dm.G
        pre_ref[...] = pre[first:first + dm.rows_of(t)]
        y = silu_masked(dm, base, k, pre, logistic(pre))
        y_ref[...] = y
        if has_mirror:
            keep = dm.fwd(dm.sections - 1 - t)
            first = (k - keep) * dm.G
            mirror_ref[...] = y[first:first + dm.rows_of(keep)]

    if t > 0:
        @pl.when(me_ref[2] != t)
        def _():
            own_ref[...] = kept_ref[...]


def split_kernel(dm, me_ref, f_ref, l_ref, *refs):
    outs, marks = refs[:dm.micro], refs[dm.micro]
    W = dm.W
    layers = f_ref.shape[0] // dm.micro
    for e in range(dm.micro):
        crop = lax.rem(me_ref[1] + e, dm.micro)
        marks[...] = jnp.zeros(marks.shape, F32)
        for layer in range(layers):
            at = crop * layers + layer
            outs[e][layer * W:(layer + 1) * W, :] = f_ref[at]
            marks[layer:layer + 1, 0:W] = l_ref[at].astype(F32)
        outs[e][layers * W:, :] = marks[...].astype(BF)


def window_kernel(dm, wing, cols, me_ref, *refs):
    crops, outs, xs = refs[:dm.micro], refs[dm.micro:-1], refs[-1]
    C, W, own = dm.C, dm.W, dm.own
    layers = dm.G // dm.slabs
    xs[0:16, :] = jnp.zeros((16, C), F32)
    xs[wing + W:, :] = jnp.zeros((xs.shape[0] - wing - W, C), F32)
    row = lax.broadcasted_iota(jnp.int32, (cols, C), 0)
    for e in range(dm.micro):
        crop = crops[e][...].astype(F32)
        core = lax.rem(me_ref[1] + (dm.micro - e), dm.micro)
        for layer in range(layers):
            xs[wing:wing + W, :] = crop[layer * W:(layer + 1) * W]
            mark = crop[layers * W + layer:layers * W + layer + 1]
            for r in range(dm.parts):
                place = lax.rem(me_ref[0] + r, dm.parts)
                start = pl.multiple_of(place * own, 8)
                value = jnp.where(row == own + 2 * wing, mark, xs[pl.ds(start, cols), :])
                outs[r][core * layers + layer] = value.astype(BF)


def gather_cells(dm, xg, xf):
    rows = (dm.own + 2 * (dm.fwd(0) + 1)) * dm.G
    cells = jnp.transpose(xg[...], (1, 0, 2))
    cells = cells.reshape(cells.shape[0] * dm.G, dm.C)
    xf[PAD:PAD + rows, :] = cells[0:rows]


def load_kernel(w_ref, b_ref, out_ref, out_b_ref):
    out_ref[...] = w_ref[...]
    out_b_ref[...] = b_ref[...]


def flip_kernel(C, w_ref, out_ref):
    for tap in range(27):
        out_ref[tap * C:(tap + 1) * C, :] = jnp.transpose(w_ref[tap * C:(tap + 1) * C, :])


def back_conv(dm, t, pg, xf, x27, wt_ref, b_ref, msg_ref):
    width = dm.own + 2 * (t - 1)
    stage(xf, pg, dm.rows_of(t))
    spread(dm, xf, x27, width, -1)
    grad = dot(x27[0:width * dm.G, :], wt_ref[...])
    if t <= dm.half:
        grad = grad + dot_nt(pg[dm.G:dm.G + width * dm.G], b_ref[...])
    msg_ref[0:width * dm.G, :] = grad.astype(BF)


def flat_labels(dm, base, width, lab_ref):
    G, cells = dm.G, width * dm.G
    lanes = dm.C
    cell = lax.broadcasted_iota(jnp.int32, (lanes, cells), 1)
    row = lax.broadcasted_iota(jnp.int32, (lanes, cells), 0)
    pick = jnp.where((cell // G + base == row) & (row < dm.W), 1.0, 0.0).astype(BF)
    found = dot(lab_ref[...].astype(BF), pick)
    g = lax.broadcasted_iota(jnp.int32, (G, cells), 1) % G
    row = lax.broadcasted_iota(jnp.int32, (G, cells), 0)
    line = jnp.sum(jnp.where(g == row, found, 0.0), axis=0, keepdims=True)
    return jnp.broadcast_to(line, (8, cells))


def affinity(dm, width, lab, off_ref):
    G, cells = dm.G, width * dm.G
    total = lab.shape[1]
    mid = lab[:, G:G + cells]
    row = lax.broadcasted_iota(jnp.int32, (8, cells), 0)
    g = lax.broadcasted_iota(jnp.int32, (8, cells), 1) % G
    d, r = g // dm.R, g % dm.R
    target = jnp.zeros((8, cells), F32)
    for j in range(dm.offs):
        dz, dy, dx = off_ref[j, 0], off_ref[j, 1], off_ref[j, 2]
        shift = G + dx * G + dz * dm.R + dy
        near = pltpu.roll(lab, lax.rem(2 * total - shift, total), 1)[:, 0:cells]
        inside = (d + dz >= 0) & (d + dz < dm.D) & (r + dy >= 0) & (r + dy < dm.R)
        same = inside & (near == mid) & (mid != 0.0) & (row == j)
        target = jnp.where(same, 1.0, target)
    return target


def target_kernel(dm, me_ref, off_ref, lab_ref, out_ref):
    t = dm.sections - 1
    lab = flat_labels(dm, me_ref[0] * dm.own - t - 1, dm.own + 2 * t + 2, lab_ref)
    out_ref[...] = affinity(dm, dm.own + 2 * t, lab, off_ref)


def last_kernel(dm, *refs):
    (me_ref, x_ref, w_ref, b_ref, skip_ref, kept_ref, wt_ref, head_ref, target_ref) = refs[:9]
    msg_ref, pgx_ref, skip_out, own_ref, xf, x27, lines = refs[9:]
    t = dm.sections - 1

    @pl.when(me_ref[2] == t)
    def _():
        base = me_ref[0] * dm.own
        G, C, own = dm.G, dm.C, dm.own
        mid, size = t * G, own * G
        own_ref[...] = x_ref[mid + G:mid + G + size, :]
        stage(xf, x_ref[...], dm.rows_of(t + 1))
        pre = preact(dm, t, xf, x27, skip_ref, w_ref, b_ref)
        gate = logistic(pre)
        y = silu_masked(dm, base, t, pre, gate)
        logits = dot_nt(head_ref[...], y)
        target = target_ref[...]
        live = lax.broadcasted_iota(jnp.int32, logits.shape, 0) < dm.offs
        sig = 1.0 / (1.0 + jnp.exp(-logits))
        lg = jnp.where(live, loss_scale * (sig - target) / dm.count, 0.0).astype(BF)
        term = jnp.maximum(logits, 0.0) + jnp.log(1.0 + jnp.exp(-jnp.abs(logits))) - target * logits
        term = jnp.where(live, term, 0.0)[:, mid:mid + size]
        loss = jnp.sum(jnp.sum(term, axis=1, keepdims=True), axis=0, keepdims=True)
        head_part = dot(lg[:, mid:mid + size], y[mid:mid + size])
        used = dm.offs + 1
        lines[...] = jnp.zeros(lines.shape, F32)
        lines[0:dm.offs, :] = head_part[0:dm.offs]
        lines[dm.offs:used, :] = jnp.broadcast_to(loss, (1, C))
        rest = lines[0:8, :]
        for i in range(3):
            piece = rest.astype(BF).astype(F32)
            lines[i * used:(i + 1) * used, :] = piece[0:used]
            rest = rest - piece
        carry = lines[...].astype(BF)
        upstream = dot_tn(lg, head_ref[...])
        pg = pre_gradient(dm, base, t, upstream, pre, gate)
        pgx_ref[0:size, :] = pg[mid:mid + size]
        pgx_ref[size:size + CARRY, :] = carry
        back_conv(dm, t, pg, xf, x27, wt_ref, b_ref, msg_ref)
        end = dm.rows_of(t - 1)
        msg_ref[end:end + CARRY, :] = carry
        m = dm.sections - 1 - t
        first = (t - m) * G
        skip_out[...] = dot_nt(pg[first:first + dm.rows_of(m)], b_ref[...]).astype(BF)

    @pl.when(me_ref[2] != t)
    def _():
        own_ref[...] = kept_ref[...]


def backward_kernel(dm, t, has_skip_in, *refs):
    refs = list(refs)
    me_ref, down_ref, pre_ref, kept_ref = refs[:4]
    at = 4
    if t > 0:
        wt_ref, b_ref = refs[at:at + 2]
        at += 2
    if has_skip_in:
        skip_ref = refs[at]
        at += 1
    pgx_ref = refs[at]
    at += 1
    if t > 0:
        msg_ref = refs[at]
        at += 1
        if t > dm.half:
            skip_out = refs[at]
            at += 1
        xf, x27 = refs[at:at + 2]

    @pl.when(me_ref[2] == t)
    def _():
        base = me_ref[0] * dm.own
        ro = dm.rows_of(t)
        upstream = down_ref[0:ro, :].astype(F32)
        if has_skip_in:
            upstream = upstream + skip_ref[0:ro, :].astype(F32)
        pre = pre_ref[...]
        pg = pre_gradient(dm, base, t, upstream, pre, logistic(pre))
        mid, size = t * dm.G, dm.own * dm.G
        carry = down_ref[ro:ro + CARRY, :]
        pgx_ref[0:size, :] = pg[mid:mid + size]
        pgx_ref[size:size + CARRY, :] = carry
        if t > 0:
            back_conv(dm, t, pg, xf, x27, wt_ref, b_ref, msg_ref)
            end = dm.rows_of(t - 1)
            msg_ref[end:end + CARRY, :] = carry
            if t > dm.half:
                m = dm.sections - 1 - t
                first = (t - m) * dm.G
                skip_out[...] = dot_nt(pg[first:first + dm.rows_of(m)], b_ref[...]).astype(BF)

    @pl.when(me_ref[2] != t)
    def _():
        pgx_ref[...] = kept_ref[...]


def turn_kernel(dm, *refs):
    q_ref = refs[0]
    x_refs = refs[1:1 + dm.slabs]
    b_refs = refs[1 + dm.slabs:1 + 2 * dm.slabs]
    xt_ref, bt_ref, xf = refs[1 + 2 * dm.slabs:]
    C, size = dm.C, dm.own * dm.G
    cells = dm.slabs * size
    for e in range(dm.micro):
        for r in range(dm.parts):
            block = e * dm.parts + r
            place = lax.rem(q_ref[0] + (dm.parts - r), dm.parts) + e * dm.parts
            at = pl.multiple_of(place * size, size)
            xf[pl.ds(PAD + at, size), :] = x_refs[block][...].astype(F32)

            @pl.when(q_ref[2] > dm.half)
            def _():
                bt_ref[:, pl.ds(at, size)] = jnp.transpose(b_refs[block][...])

    for kz in range(3):
        for ky in range(3):
            delta = (kz - 1) * dm.R + ky - 1
            part = xf[PAD + delta:PAD + delta + cells, :]
            if kz != 1 or ky != 1:
                part = part.reshape(cells // dm.G, dm.G, C)
                part = jnp.where(group_mask(dm, kz - 1, ky - 1), part, 0.0).reshape(cells, C)
            tap = kz * 3 + ky
            xt_ref[tap * C:(tap + 1) * C, :] = jnp.transpose(part.astype(BF))


def weight_kernel(dm, *refs):
    q_ref, xt_ref, bt_ref = refs[:3]
    blocks = refs[3:3 + dm.slabs]
    grad_ref, mix_ref, head_ref, loss_ref, full, held, sums, sems = refs[3 + dm.slabs:]
    G, C, W = dm.G, dm.C, dm.W
    size = dm.own * G
    span = (W + 2) * G
    cells = W * G
    for e in range(dm.micro):
        start = e * span
        full[start:start + G, :] = jnp.zeros((G, C), BF)
        full[start + (W + 1) * G:start + span, :] = jnp.zeros((G, C), BF)
        for r in range(dm.parts):
            block = blocks[e * dm.parts + r]
            place = lax.rem(q_ref[0] + (dm.parts - r), dm.parts)
            at = pl.multiple_of(start + G + place * size, 16)
            full[pl.ds(at, size), :] = block[0:size, :]
            carry = block[size:size + CARRY, :].astype(F32)
            slot = lax.rem(q_ref[1] + (dm.micro - e), dm.micro) * dm.parts + place
            used = dm.offs + 1
            sums[slot, 0:used] = (carry[0:used] + carry[used:2 * used]) + carry[2 * used:3 * used]

    def product(lhs_ref, row, count, kx):
        total = None
        for e in range(dm.micro):
            first = e * span + (2 - kx) * G
            one = dot(lhs_ref[row:row + count, e * cells:(e + 1) * cells], full[first:first + cells, :])
            total = one if total is None else total + one
        return total

    copies = []
    for step in range(27):
        kx, tap = step // 9, step % 9
        held[step] = product(xt_ref, tap * C, C, kx)
        copies.append(pltpu.make_async_copy(held.at[step], grad_ref.at[tap, kx], sems.at[step]))
        copies[step].start()

    @pl.when(q_ref[2] > dm.half)
    def _():
        mix_ref[...] = product(bt_ref, 0, C, 1)

    @pl.when(q_ref[2] <= dm.half)
    def _():
        mix_ref[...] = held[13]

    total = jnp.zeros((8, C), F32)
    for slot in range(dm.slabs):
        total = total + sums[slot]
    head_ref[...] = total[0:dm.offs]
    loss_ref[...] = total[dm.offs:dm.offs + 1, 0:1] / dm.count
    for copy in copies:
        copy.wait()


def whole():
    return pl.BlockSpec(memory_space=pltpu.VMEM)


def scalar():
    return pl.BlockSpec(memory_space=pltpu.SMEM)


def shape(rows, cols, kind):
    return jax.ShapeDtypeStruct((rows, cols), kind)


def nbytes(arrays):
    return sum(math.prod(a.shape) * jnp.dtype(a.dtype).itemsize for a in arrays)


def call(kernel, scalars, operands, outs, scratch, flops, places=None):
    moved = nbytes(operands) + nbytes(outs)
    room = moved + nbytes([a for a in scratch if a.dtype in (BF, F32)]) + SPARE
    return pl.pallas_call(
        kernel,
        out_shape=outs,
        in_specs=[scalar()] * len(scalars) + [whole()] * len(operands),
        out_specs=places or [whole()] * len(outs),
        scratch_shapes=scratch,
        compiler_params=pltpu.CompilerParams(vmem_limit_bytes=room),
        cost_estimate=pl.CostEstimate(flops=flops, bytes_accessed=moved, transcendentals=0),
    )(*scalars, *operands)


def conv_scratch(dm, rin, ro):
    return [
        pltpu.VMEM((rin + 2 * PAD, dm.C), F32),
        pltpu.VMEM((ro, 27 * dm.C), BF),
    ]


def body(features_in, labels, offsets, conv_weight, branch_weight, head_weight):
    n = lax.axis_size("section")
    slabs = lax.axis_size("slab")
    micro, C, thick, R, W = features_in.shape
    dm = Dims(n, slabs, micro, C, thick * slabs, R, W, offsets.shape[0])
    G, own, parts, half = dm.G, dm.own, dm.parts, dm.half
    section = lax.axis_index("section")
    slab = lax.axis_index("slab")
    c, q = lax.rem(slab, micro), lax.div(slab, micro)
    me = jnp.stack([q, c, section]).astype(jnp.int32)
    size = own * G

    def hop(x, source, target):
        return lax.ppermute(x, "section", [(source, target)])

    def rotate(x, r):
        pairs = [(p * micro + e, ((p + r) % parts) * micro + e) for p in range(parts) for e in range(micro)]
        return lax.ppermute(x, "slab", pairs)

    def swap(x, e):
        pairs = [(p * micro + i, p * micro + (i + e) % micro) for p in range(parts) for i in range(micro)]
        return lax.ppermute(x, "slab", pairs)

    def gather(block, lowest):
        found = [block]
        for r in range(1, parts):
            pairs = [(p * micro + e, (p + r) % parts * micro + e) for p in range(parts) for e in range(micro)]
            found.append(along(block, pairs, lowest))
        blocks = list(found)
        for e in range(1, micro):
            pairs = [(p * micro + i, p * micro + (i + e) % micro) for p in range(parts) for i in range(micro)]
            blocks += [along(b, pairs, lowest) for b in found]
        return blocks

    def along(x, pairs, lowest):
        joint = [(s * slabs + i, s * slabs + j) for s in range(lowest, n) for i, j in pairs]
        return lax.ppermute(x, ("section", "slab"), joint)

    source = conv_weight[0].reshape(27 * C, C)
    kernel, mixing = call(
        load_kernel, [], [source, branch_weight[0]],
        [shape(27 * C, C, BF), shape(C, C, BF)], [], 0,
    )

    wing = dm.fwd(0) + 1
    wide = own + 2 * wing
    cols = -(-(wide + 1) // 16) * 16
    layers = thick * R
    cells = jnp.transpose(features_in, (0, 2, 3, 4, 1)).reshape(micro * layers, W, C)
    lines = -(-layers // 16) * 16
    crops = list(call(
        functools.partial(split_kernel, dm),
        [me], [cells, labels.reshape(micro * layers, 1, W)],
        [shape(layers * W + lines, C, BF)] * micro,
        [pltpu.VMEM((lines, C), F32)],
        1000,
    ))
    for e in range(1, micro):
        crops[e] = swap(crops[e], e)
    windows = call(
        functools.partial(window_kernel, dm, wing, cols),
        [me], crops,
        [jax.ShapeDtypeStruct((micro * layers, cols, C), BF)] * parts,
        [pltpu.VMEM((-(-(wing + W + cols) // 8) * 8, C), F32)],
        1000,
    )
    current = [windows[0]]
    for r in range(1, parts):
        current.append(rotate(windows[r], r))

    head = jnp.pad(jnp.transpose(head_weight), ((0, 8 - dm.offs), (0, 0)))

    pres, mirrors = [], {}
    kept = kernel_t = None
    for t in range(n - 1):
        k = dm.fwd(t)
        has_skip, has_mirror = t > half, t < half - 1
        operands = [*(current if t == 0 else [current]), kernel, mixing]
        if has_skip:
            operands.append(mirrors[t])
        if t > 0:
            operands.append(kept)
        outs = [shape(dm.rows_of(k), C, BF), shape(dm.rows_of(t), C, F32), shape(size, C, BF)]
        scratch = conv_scratch(dm, dm.rows_of(k + 1), dm.rows_of(k))
        if has_mirror:
            outs.append(shape(dm.rows_of(dm.fwd(n - 1 - t)), C, BF))
        if t == 0:
            outs.append(shape(G, C, F32))
            scratch.append(pltpu.VMEM((G, cols, C), F32))
        results = call(
            functools.partial(forward_kernel, dm, t, has_skip, has_mirror),
            [me], operands, outs, scratch,
            2 * dm.rows_of(k) * 28 * C * C,
        )
        pres.append(results[1])
        kept = results[2]
        current = hop(results[0], t, t + 1)
        if t == 0:
            marks = results[-1]
            raw, marks, _ = lax.optimization_barrier((kernel, marks, results[0]))
            targets = call(
                functools.partial(target_kernel, dm), [me, offsets], [marks],
                [shape(8, dm.rows_of(n - 1), F32)], [], 1000,
            )[0]
            kernel_t = call(
                functools.partial(flip_kernel, C), [], [raw],
                [shape(27 * C, C, BF)], [], 2 * 27 * C * C * 100,
            )[0]
        if has_mirror:
            later, current = lax.optimization_barrier((results[3], current))
            mirrors[n - 1 - t] = hop(later, t, n - 1 - t)

    t = n - 1
    skip = mirrors[t]
    branch = skip[t * G:t * G + size]
    for s in range(half + 1, n - 1):
        first = dm.fwd(s) * G
        branch = jnp.where(section == s, mirrors[s][first:first + size], branch)
    branch, _ = lax.optimization_barrier((branch, results[0]))
    branches = gather(branch, 0)
    outs = [
        shape(dm.rows_of(t - 1) + CARRY, C, BF),
        shape(size + CARRY, C, BF),
        shape(dm.rows_of(0), C, BF),
        shape(size, C, BF),
    ]
    results = call(
        functools.partial(last_kernel, dm),
        [me],
        [current, kernel, mixing, skip, kept, kernel_t, head, targets],
        outs,
        conv_scratch(dm, dm.rows_of(t + 1), dm.rows_of(t)) + [pltpu.VMEM((CARRY, C), F32)],
        4 * dm.rows_of(t) * 28 * C * C,
    )
    down = hop(results[0], t, t - 1)
    block, held = results[1], results[3]
    skip_grads = {0: hop(results[2], t, 0)}
    held = gather(held, 0)
    cells_all = micro * W * G

    for t in range(n - 2, -1, -1):
        has_skip = t < half - 1
        operands = [down, pres[t], block]
        if t > 0:
            operands += [kernel_t, mixing]
        if has_skip:
            operands.append(skip_grads[t])
        outs = [shape(size + CARRY, C, BF)]
        scratch = []
        if t > 0:
            outs.append(shape(dm.rows_of(t - 1) + CARRY, C, BF))
            if t > half:
                outs.append(shape(dm.rows_of(n - 1 - t), C, BF))
            scratch = conv_scratch(dm, dm.rows_of(t), dm.rows_of(t - 1))
        results = call(
            functools.partial(backward_kernel, dm, t, has_skip),
            [me], operands, outs, scratch,
            2 * dm.rows_of(max(t - 1, 0)) * 28 * C * C if t > 0 else 1000,
        )
        block = results[0]
        if t > 0:
            down = hop(results[1], t, t - 1)
            if t > half:
                skip_grads[n - 1 - t] = hop(results[2], t, n - 1 - t)

    held[0], _ = lax.optimization_barrier((held[0], block))
    xt, bt = call(
        functools.partial(turn_kernel, dm),
        [me], held + branches,
        [shape(9 * C, cells_all, BF), shape(C, cells_all, BF)],
        [pltpu.VMEM((cells_all + 2 * PAD, C), F32)],
        2 * 10 * cells_all * C * 100,
    )
    near = [block] + [rotate(block, r) for r in range(1, parts)]
    *far, xt = lax.optimization_barrier((*near[1:], xt))
    near = [block] + far
    blocks = list(near)
    for e in range(1, micro):
        blocks += [swap(b, e) for b in near]
    operands = [xt, bt, *blocks]
    scratch = [
        pltpu.VMEM((micro * (W + 2) * G, C), BF),
        pltpu.VMEM((27, C, C), F32),
        pltpu.VMEM((slabs, 8, C), F32),
        pltpu.SemaphoreType.DMA((27,)),
    ]
    outs = [
        jax.ShapeDtypeStruct((9, 3, C, C), F32),
        shape(C, C, F32),
        shape(dm.offs, C, F32),
        shape(1, 1, F32),
    ]
    moved = nbytes(operands) + nbytes(outs)
    grad, mix, heads, loss = pl.pallas_call(
        functools.partial(weight_kernel, dm),
        name="weights",
        out_shape=outs,
        in_specs=[scalar()] + [whole()] * len(operands),
        out_specs=[pl.BlockSpec(memory_space=pl.ANY), whole(), whole(), whole()],
        scratch_shapes=scratch,
        compiler_params=pltpu.CompilerParams(
            vmem_limit_bytes=nbytes(operands) + nbytes(scratch[:3]) + SPARE
        ),
        cost_estimate=pl.CostEstimate(
            flops=2 * cells_all * 28 * C * C, bytes_accessed=moved, transcendentals=0
        ),
    )(me, *operands)
    return (
        loss[0, 0],
        grad.reshape((1, 3, 3, 3, C, C)),
        mix[None],
        jnp.transpose(heads),
    )


def solution(mesh):
    placed = (
        P(None, None, "slab", None, None),
        P(None, "slab", None, None),
        P(),
        P("section", None, None, None, None, None),
        P("section", None, None),
        P(),
    )
    return jax.shard_map(
        body,
        mesh=mesh,
        in_specs=placed,
        out_specs=(P(), P("section", None, None, None, None, None), P("section", None, None), P()),
        check_vma=False,
    )
```

```python
import functools
import math

import jax
import jax.numpy as jnp
from jax import lax
from jax.experimental import pallas as pl
from jax.experimental.pallas import tpu as pltpu
from jax.sharding import PartitionSpec as P


loss_scale = 1024.0
BF = jnp.bfloat16
F32 = jnp.float32
PAD = 8
SPARE = 6 * 1024 * 1024
CARRY = 16


class Dims:
    def __init__(self, sections, slabs, micro, channels, depth, rows, cols, offs):
        self.sections, self.half = sections, sections // 2
        self.slabs, self.micro = slabs, micro
        self.C, self.D, self.R, self.W, self.offs = channels, depth, rows, cols, offs
        self.G = depth * rows
        self.parts = slabs // micro
        self.own = cols // self.parts
        self.count = micro * offs * depth * rows * cols

    def fwd(self, t):
        return 2 * (self.sections - 1) - t

    def rows_of(self, k):
        return (self.own + 2 * k) * self.G


def group_mask(dm, kz, ky):
    g = lax.broadcasted_iota(jnp.int32, (1, dm.G, dm.C), 1)
    d = g // dm.R + kz
    r = g % dm.R + ky
    return (d >= 0) & (d < dm.D) & (r >= 0) & (r < dm.R)


def column_mask(dm, base, k, width):
    col = lax.broadcasted_iota(jnp.int32, (width, dm.G, dm.C), 0) + (base - k)
    return (col >= 0) & (col < dm.W)


def spread(dm, xf, x27, width, sign):
    G, C = dm.G, dm.C
    rin = (width + 2) * G
    for kz in range(3):
        for ky in range(3):
            dz, dy = sign * (kz - 1), sign * (ky - 1)
            delta = dz * dm.R + dy
            part = xf[PAD + delta:PAD + delta + rin, :]
            if kz != 1 or ky != 1:
                part = part.reshape(width + 2, G, C)
                part = jnp.where(group_mask(dm, dz, dy), part, 0.0).reshape(rin, C)
            part = part.astype(BF)
            for kx in range(3):
                first = (1 + sign * (kx - 1)) * G
                tap = (kz * 3 + ky) * 3 + kx
                x27[0:width * G, tap * C:(tap + 1) * C] = part[first:first + width * G]


def dot(a, b):
    return lax.dot_general(a, b, (((1,), (0,)), ((), ())), preferred_element_type=F32)


def dot_nt(a, b):
    return lax.dot_general(a, b, (((1,), (1,)), ((), ())), preferred_element_type=F32)


def dot_tn(a, b):
    return lax.dot_general(a, b, (((0,), (0,)), ((), ())), preferred_element_type=F32)


def stage(xf, x, rin):
    xf[PAD:PAD + rin, :] = x.astype(F32)


def preact(dm, t, xf, x27, skip_ref, w_ref, b_ref):
    width = dm.own + 2 * dm.fwd(t)
    ro = width * dm.G
    spread(dm, xf, x27, width, 1)
    if t <= dm.half:
        branch = x27[0:ro, 13 * dm.C:14 * dm.C]
    else:
        branch = skip_ref[0:ro, :]
    return dot(x27[0:ro, :], w_ref[...]) + dot(branch, b_ref[...])


def silu_masked(dm, base, k, pre):
    width = dm.own + 2 * k
    value = pre * (1.0 / (1.0 + jnp.exp(-pre)))
    value = value.reshape(width, dm.G, dm.C)
    value = jnp.where(column_mask(dm, base, k, width), value, 0.0)
    return value.reshape(width * dm.G, dm.C).astype(BF)


def pre_gradient(dm, base, k, upstream, pre):
    width = dm.own + 2 * k
    sig = 1.0 / (1.0 + jnp.exp(-pre))
    value = upstream * (sig * (1.0 + pre * (1.0 - sig)))
    value = value.reshape(width, dm.G, dm.C)
    value = jnp.where(column_mask(dm, base, k, width), value, 0.0)
    return value.reshape(width * dm.G, dm.C).astype(BF)


def forward_kernel(dm, t, has_skip_in, has_mirror, *refs):
    refs = list(refs)
    count = dm.parts if t == 0 else 1
    me_ref, x_refs = refs[0], refs[1:1 + count]
    w_ref, b_ref = refs[1 + count:3 + count]
    at = 3 + count
    x_ref = x_refs[0]
    skip_ref = kept_ref = None
    if has_skip_in:
        skip_ref = refs[at]
        at += 1
    if t > 0:
        kept_ref = refs[at]
        at += 1
    y_ref, pre_ref, own_ref = refs[at:at + 3]
    at += 3
    if has_mirror:
        mirror_ref = refs[at]
        at += 1
    if t == 0:
        lab_ref, xg = refs[at], refs[-1]
        at += 1
        wide = dm.own + 2 * (dm.fwd(0) + 1)
        layers = dm.G // dm.parts
        for r in range(dm.parts):
            place = lax.rem(me_ref[0] + (dm.parts - r), dm.parts)
            xg[pl.ds(place * layers, layers)] = x_refs[r][...].astype(F32)
        lab_ref[...] = xg[:, wide, :]
    xf, x27 = refs[at:at + 2]

    @pl.when(me_ref[2] == t)
    def _():
        base = me_ref[0] * dm.own
        k = dm.fwd(t)
        if t == 0:
            gather_cells(dm, xg, xf)
        else:
            stage(xf, x_ref[...], dm.rows_of(k + 1))
        size, mid = dm.own * dm.G, (k + 1) * dm.G
        own_ref[...] = xf[PAD + mid:PAD + mid + size, :].astype(BF)
        pre = preact(dm, t, xf, x27, skip_ref, w_ref, b_ref)
        first = (k - t) * dm.G
        pre_ref[...] = pre[first:first + dm.rows_of(t)]
        y = silu_masked(dm, base, k, pre)
        y_ref[...] = y
        if has_mirror:
            keep = dm.fwd(dm.sections - 1 - t)
            first = (k - keep) * dm.G
            mirror_ref[...] = y[first:first + dm.rows_of(keep)]

    if t > 0:
        @pl.when(me_ref[2] != t)
        def _():
            own_ref[...] = kept_ref[...]


def split_kernel(dm, me_ref, f_ref, l_ref, *refs):
    outs, marks = refs[:dm.micro], refs[dm.micro]
    W = dm.W
    layers = f_ref.shape[0] // dm.micro
    for e in range(dm.micro):
        crop = lax.rem(me_ref[1] + e, dm.micro)
        marks[...] = jnp.zeros(marks.shape, F32)
        for layer in range(layers):
            at = crop * layers + layer
            outs[e][layer * W:(layer + 1) * W, :] = f_ref[at]
            marks[layer:layer + 1, 0:W] = l_ref[at].astype(F32)
        outs[e][layers * W:, :] = marks[...].astype(BF)


def window_kernel(dm, wing, cols, me_ref, *refs):
    crops, outs, xs = refs[:dm.micro], refs[dm.micro:-1], refs[-1]
    C, W, own = dm.C, dm.W, dm.own
    layers = dm.G // dm.slabs
    xs[0:16, :] = jnp.zeros((16, C), F32)
    xs[wing + W:, :] = jnp.zeros((xs.shape[0] - wing - W, C), F32)
    row = lax.broadcasted_iota(jnp.int32, (cols, C), 0)
    for e in range(dm.micro):
        crop = crops[e][...].astype(F32)
        core = lax.rem(me_ref[1] + (dm.micro - e), dm.micro)
        for layer in range(layers):
            xs[wing:wing + W, :] = crop[layer * W:(layer + 1) * W]
            mark = crop[layers * W + layer:layers * W + layer + 1]
            for r in range(dm.parts):
                place = lax.rem(me_ref[0] + r, dm.parts)
                start = pl.multiple_of(place * own, 8)
                value = jnp.where(row == own + 2 * wing, mark, xs[pl.ds(start, cols), :])
                outs[r][core * layers + layer] = value.astype(BF)


def gather_cells(dm, xg, xf):
    rows = (dm.own + 2 * (dm.fwd(0) + 1)) * dm.G
    cells = jnp.transpose(xg[...], (1, 0, 2))
    cells = cells.reshape(cells.shape[0] * dm.G, dm.C)
    xf[PAD:PAD + rows, :] = cells[0:rows]


def load_kernel(chunks, w_ref, b_ref, out_ref, out_b_ref, sems):
    rows = w_ref.shape[0] // chunks
    copies = []
    for i in range(chunks):
        part = pl.ds(i * rows, rows)
        copies.append(pltpu.make_async_copy(w_ref.at[part], out_ref.at[part], sems.at[i]))
        copies[i].start()
    copies.append(pltpu.make_async_copy(b_ref, out_b_ref, sems.at[chunks]))
    copies[chunks].start()
    for copy in copies:
        copy.wait()


def flip_kernel(C, w_ref, out_ref):
    for tap in range(27):
        out_ref[tap * C:(tap + 1) * C, :] = jnp.transpose(w_ref[tap * C:(tap + 1) * C, :])


def back_conv(dm, t, pg, xf, x27, wt_ref, b_ref, msg_ref):
    width = dm.own + 2 * (t - 1)
    stage(xf, pg, dm.rows_of(t))
    spread(dm, xf, x27, width, -1)
    grad = dot(x27[0:width * dm.G, :], wt_ref[...])
    if t <= dm.half:
        grad = grad + dot_nt(pg[dm.G:dm.G + width * dm.G], b_ref[...])
    msg_ref[0:width * dm.G, :] = grad.astype(BF)


def flat_labels(dm, base, width, lab_ref):
    G, cells = dm.G, width * dm.G
    lanes = dm.C
    cell = lax.broadcasted_iota(jnp.int32, (lanes, cells), 1)
    row = lax.broadcasted_iota(jnp.int32, (lanes, cells), 0)
    pick = jnp.where((cell // G + base == row) & (row < dm.W), 1.0, 0.0).astype(BF)
    found = dot(lab_ref[...].astype(BF), pick)
    g = lax.broadcasted_iota(jnp.int32, (G, cells), 1) % G
    row = lax.broadcasted_iota(jnp.int32, (G, cells), 0)
    line = jnp.sum(jnp.where(g == row, found, 0.0), axis=0, keepdims=True)
    return jnp.broadcast_to(line, (8, cells))


def affinity(dm, width, lab, off_ref):
    G, cells = dm.G, width * dm.G
    total = lab.shape[1]
    mid = lab[:, G:G + cells]
    row = lax.broadcasted_iota(jnp.int32, (8, cells), 0)
    g = lax.broadcasted_iota(jnp.int32, (8, cells), 1) % G
    d, r = g // dm.R, g % dm.R
    target = jnp.zeros((8, cells), F32)
    for j in range(dm.offs):
        dz, dy, dx = off_ref[j, 0], off_ref[j, 1], off_ref[j, 2]
        shift = G + dx * G + dz * dm.R + dy
        near = pltpu.roll(lab, lax.rem(2 * total - shift, total), 1)[:, 0:cells]
        inside = (d + dz >= 0) & (d + dz < dm.D) & (r + dy >= 0) & (r + dy < dm.R)
        same = inside & (near == mid) & (mid != 0.0) & (row == j)
        target = jnp.where(same, 1.0, target)
    return target


def target_kernel(dm, me_ref, off_ref, lab_ref, out_ref):
    t = dm.sections - 1
    lab = flat_labels(dm, me_ref[0] * dm.own - t - 1, dm.own + 2 * t + 2, lab_ref)
    out_ref[...] = affinity(dm, dm.own + 2 * t, lab, off_ref)


def last_kernel(dm, *refs):
    (me_ref, x_ref, w_ref, b_ref, skip_ref, kept_ref, wt_ref, head_ref, target_ref) = refs[:9]
    msg_ref, pgx_ref, skip_out, own_ref, xf, x27, lines = refs[9:]
    t = dm.sections - 1

    @pl.when(me_ref[2] == t)
    def _():
        base = me_ref[0] * dm.own
        G, C, own = dm.G, dm.C, dm.own
        mid, size = t * G, own * G
        own_ref[...] = x_ref[mid + G:mid + G + size, :]
        stage(xf, x_ref[...], dm.rows_of(t + 1))
        pre = preact(dm, t, xf, x27, skip_ref, w_ref, b_ref)
        y = silu_masked(dm, base, t, pre)
        logits = dot_nt(head_ref[...], y)
        target = target_ref[...]
        live = lax.broadcasted_iota(jnp.int32, logits.shape, 0) < dm.offs
        sig = 1.0 / (1.0 + jnp.exp(-logits))
        lg = jnp.where(live, loss_scale * (sig - target) / dm.count, 0.0).astype(BF)
        term = jnp.maximum(logits, 0.0) + jnp.log(1.0 + jnp.exp(-jnp.abs(logits))) - target * logits
        term = jnp.where(live, term, 0.0)[:, mid:mid + size]
        loss = jnp.sum(jnp.sum(term, axis=1, keepdims=True), axis=0, keepdims=True)
        head_part = dot(lg[:, mid:mid + size], y[mid:mid + size])
        used = dm.offs + 1
        lines[...] = jnp.zeros(lines.shape, F32)
        lines[0:dm.offs, :] = head_part[0:dm.offs]
        lines[dm.offs:used, :] = jnp.broadcast_to(loss, (1, C))
        rest = lines[0:8, :]
        for i in range(3):
            piece = rest.astype(BF).astype(F32)
            lines[i * used:(i + 1) * used, :] = piece[0:used]
            rest = rest - piece
        carry = lines[...].astype(BF)
        upstream = dot_tn(lg, head_ref[...])
        pg = pre_gradient(dm, base, t, upstream, pre)
        pgx_ref[0:size, :] = pg[mid:mid + size]
        pgx_ref[size:size + CARRY, :] = carry
        back_conv(dm, t, pg, xf, x27, wt_ref, b_ref, msg_ref)
        end = dm.rows_of(t - 1)
        msg_ref[end:end + CARRY, :] = carry
        m = dm.sections - 1 - t
        first = (t - m) * G
        skip_out[...] = dot_nt(pg[first:first + dm.rows_of(m)], b_ref[...]).astype(BF)

    @pl.when(me_ref[2] != t)
    def _():
        own_ref[...] = kept_ref[...]


def backward_kernel(dm, t, has_skip_in, *refs):
    refs = list(refs)
    me_ref, down_ref, pre_ref, kept_ref = refs[:4]
    at = 4
    if t > 0:
        wt_ref, b_ref = refs[at:at + 2]
        at += 2
    if has_skip_in:
        skip_ref = refs[at]
        at += 1
    pgx_ref = refs[at]
    at += 1
    if t > 0:
        msg_ref = refs[at]
        at += 1
        if t > dm.half:
            skip_out = refs[at]
            at += 1
        xf, x27 = refs[at:at + 2]

    @pl.when(me_ref[2] == t)
    def _():
        base = me_ref[0] * dm.own
        ro = dm.rows_of(t)
        upstream = down_ref[0:ro, :].astype(F32)
        if has_skip_in:
            upstream = upstream + skip_ref[0:ro, :].astype(F32)
        pg = pre_gradient(dm, base, t, upstream, pre_ref[...])
        mid, size = t * dm.G, dm.own * dm.G
        carry = down_ref[ro:ro + CARRY, :]
        pgx_ref[0:size, :] = pg[mid:mid + size]
        pgx_ref[size:size + CARRY, :] = carry
        if t > 0:
            back_conv(dm, t, pg, xf, x27, wt_ref, b_ref, msg_ref)
            end = dm.rows_of(t - 1)
            msg_ref[end:end + CARRY, :] = carry
            if t > dm.half:
                m = dm.sections - 1 - t
                first = (t - m) * dm.G
                skip_out[...] = dot_nt(pg[first:first + dm.rows_of(m)], b_ref[...]).astype(BF)

    @pl.when(me_ref[2] != t)
    def _():
        pgx_ref[...] = kept_ref[...]


def turn_kernel(dm, *refs):
    q_ref = refs[0]
    x_refs = refs[1:1 + dm.slabs]
    b_refs = refs[1 + dm.slabs:1 + 2 * dm.slabs]
    xt_ref, bt_ref, xf = refs[1 + 2 * dm.slabs:]
    C, size = dm.C, dm.own * dm.G
    cells = dm.slabs * size
    for e in range(dm.micro):
        for r in range(dm.parts):
            block = e * dm.parts + r
            place = lax.rem(q_ref[0] + (dm.parts - r), dm.parts) + e * dm.parts
            at = pl.multiple_of(place * size, size)
            xf[pl.ds(PAD + at, size), :] = x_refs[block][...].astype(F32)

            @pl.when(q_ref[2] > dm.half)
            def _():
                bt_ref[:, pl.ds(at, size)] = jnp.transpose(b_refs[block][...])

    for kz in range(3):
        for ky in range(3):
            delta = (kz - 1) * dm.R + ky - 1
            part = xf[PAD + delta:PAD + delta + cells, :]
            if kz != 1 or ky != 1:
                part = part.reshape(cells // dm.G, dm.G, C)
                part = jnp.where(group_mask(dm, kz - 1, ky - 1), part, 0.0).reshape(cells, C)
            tap = kz * 3 + ky
            xt_ref[tap * C:(tap + 1) * C, :] = jnp.transpose(part.astype(BF))


def weight_kernel(dm, *refs):
    q_ref, xt_ref, bt_ref = refs[:3]
    blocks = refs[3:3 + dm.slabs]
    grad_ref, mix_ref, head_ref, loss_ref, full, held, sums, sems = refs[3 + dm.slabs:]
    G, C, W = dm.G, dm.C, dm.W
    size = dm.own * G
    span = (W + 2) * G
    cells = W * G
    for e in range(dm.micro):
        start = e * span
        full[start:start + G, :] = jnp.zeros((G, C), BF)
        full[start + (W + 1) * G:start + span, :] = jnp.zeros((G, C), BF)
        for r in range(dm.parts):
            block = blocks[e * dm.parts + r]
            place = lax.rem(q_ref[0] + (dm.parts - r), dm.parts)
            at = pl.multiple_of(start + G + place * size, 16)
            full[pl.ds(at, size), :] = block[0:size, :]
            carry = block[size:size + CARRY, :].astype(F32)
            slot = lax.rem(q_ref[1] + (dm.micro - e), dm.micro) * dm.parts + place
            used = dm.offs + 1
            sums[slot, 0:used] = (carry[0:used] + carry[used:2 * used]) + carry[2 * used:3 * used]

    def product(lhs_ref, row, count, kx):
        total = None
        for e in range(dm.micro):
            first = e * span + (2 - kx) * G
            one = dot(lhs_ref[row:row + count, e * cells:(e + 1) * cells], full[first:first + cells, :])
            total = one if total is None else total + one
        return total

    copies = []
    for step in range(27):
        kx, tap = step // 9, step % 9
        held[step] = product(xt_ref, tap * C, C, kx)
        copies.append(pltpu.make_async_copy(held.at[step], grad_ref.at[tap, kx], sems.at[step]))
        copies[step].start()

    @pl.when(q_ref[2] > dm.half)
    def _():
        mix_ref[...] = product(bt_ref, 0, C, 1)

    @pl.when(q_ref[2] <= dm.half)
    def _():
        mix_ref[...] = held[13]

    total = jnp.zeros((8, C), F32)
    for slot in range(dm.slabs):
        total = total + sums[slot]
    head_ref[...] = total[0:dm.offs]
    loss_ref[...] = total[dm.offs:dm.offs + 1, 0:1] / dm.count
    for copy in copies:
        copy.wait()


def whole():
    return pl.BlockSpec(memory_space=pltpu.VMEM)


def scalar():
    return pl.BlockSpec(memory_space=pltpu.SMEM)


def shape(rows, cols, kind):
    return jax.ShapeDtypeStruct((rows, cols), kind)


def nbytes(arrays):
    return sum(math.prod(a.shape) * jnp.dtype(a.dtype).itemsize for a in arrays)


def call(kernel, scalars, operands, outs, scratch, flops, places=None):
    moved = nbytes(operands) + nbytes(outs)
    room = moved + nbytes([a for a in scratch if a.dtype in (BF, F32)]) + SPARE
    return pl.pallas_call(
        kernel,
        out_shape=outs,
        in_specs=[scalar()] * len(scalars) + [whole()] * len(operands),
        out_specs=places or [whole()] * len(outs),
        scratch_shapes=scratch,
        compiler_params=pltpu.CompilerParams(vmem_limit_bytes=room),
        cost_estimate=pl.CostEstimate(flops=flops, bytes_accessed=moved, transcendentals=0),
    )(*scalars, *operands)


def conv_scratch(dm, rin, ro):
    return [
        pltpu.VMEM((rin + 2 * PAD, dm.C), F32),
        pltpu.VMEM((ro, 27 * dm.C), BF),
    ]


def body(features_in, labels, offsets, conv_weight, branch_weight, head_weight):
    n = lax.axis_size("section")
    slabs = lax.axis_size("slab")
    micro, C, thick, R, W = features_in.shape
    dm = Dims(n, slabs, micro, C, thick * slabs, R, W, offsets.shape[0])
    G, own, parts, half = dm.G, dm.own, dm.parts, dm.half
    section = lax.axis_index("section")
    slab = lax.axis_index("slab")
    c, q = lax.rem(slab, micro), lax.div(slab, micro)
    me = jnp.stack([q, c, section]).astype(jnp.int32)
    size = own * G

    def hop(x, source, target):
        return lax.ppermute(x, "section", [(source, target)])

    def rotate(x, r):
        pairs = [(p * micro + e, ((p + r) % parts) * micro + e) for p in range(parts) for e in range(micro)]
        return lax.ppermute(x, "slab", pairs)

    def swap(x, e):
        pairs = [(p * micro + i, p * micro + (i + e) % micro) for p in range(parts) for i in range(micro)]
        return lax.ppermute(x, "slab", pairs)

    def gather(block, lowest):
        found = [block]
        for r in range(1, parts):
            pairs = [(p * micro + e, (p + r) % parts * micro + e) for p in range(parts) for e in range(micro)]
            found.append(along(block, pairs, lowest))
        blocks = list(found)
        for e in range(1, micro):
            pairs = [(p * micro + i, p * micro + (i + e) % micro) for p in range(parts) for i in range(micro)]
            blocks += [along(b, pairs, lowest) for b in found]
        return blocks

    def along(x, pairs, lowest):
        joint = [(s * slabs + i, s * slabs + j) for s in range(lowest, n) for i, j in pairs]
        return lax.ppermute(x, ("section", "slab"), joint)

    source = conv_weight[0].reshape(27 * C, C)
    held_hbm = pl.BlockSpec(memory_space=pltpu.HBM)
    kernel, mixing = pl.pallas_call(
        functools.partial(load_kernel, 9),
        name="load",
        out_shape=[shape(27 * C, C, BF), shape(C, C, BF)],
        in_specs=[held_hbm, held_hbm],
        out_specs=[whole(), whole()],
        scratch_shapes=[pltpu.SemaphoreType.DMA((10,))],
        compiler_params=pltpu.CompilerParams(vmem_limit_bytes=27 * C * C * 2 + SPARE),
        cost_estimate=pl.CostEstimate(flops=0, bytes_accessed=27 * C * C * 4, transcendentals=0),
    )(source, branch_weight[0])

    wing = dm.fwd(0) + 1
    wide = own + 2 * wing
    cols = -(-(wide + 1) // 16) * 16
    layers = thick * R
    cells = jnp.transpose(features_in, (0, 2, 3, 4, 1)).reshape(micro * layers, W, C)
    lines = -(-layers // 16) * 16
    crops = list(call(
        functools.partial(split_kernel, dm),
        [me], [cells, labels.reshape(micro * layers, 1, W)],
        [shape(layers * W + lines, C, BF)] * micro,
        [pltpu.VMEM((lines, C), F32)],
        1000,
    ))
    for e in range(1, micro):
        crops[e] = swap(crops[e], e)
    windows = call(
        functools.partial(window_kernel, dm, wing, cols),
        [me], crops,
        [jax.ShapeDtypeStruct((micro * layers, cols, C), BF)] * parts,
        [pltpu.VMEM((-(-(wing + W + cols) // 8) * 8, C), F32)],
        1000,
    )
    current = [windows[0]]
    for r in range(1, parts):
        current.append(rotate(windows[r], r))

    head = jnp.pad(jnp.transpose(head_weight), ((0, 8 - dm.offs), (0, 0)))

    pres, mirrors = [], {}
    kept = kernel_t = None
    for t in range(n - 1):
        k = dm.fwd(t)
        has_skip, has_mirror = t > half, t < half - 1
        operands = [*(current if t == 0 else [current]), kernel, mixing]
        if has_skip:
            operands.append(mirrors[t])
        if t > 0:
            operands.append(kept)
        outs = [shape(dm.rows_of(k), C, BF), shape(dm.rows_of(t), C, F32), shape(size, C, BF)]
        scratch = conv_scratch(dm, dm.rows_of(k + 1), dm.rows_of(k))
        if has_mirror:
            outs.append(shape(dm.rows_of(dm.fwd(n - 1 - t)), C, BF))
        if t == 0:
            outs.append(shape(G, C, F32))
            scratch.append(pltpu.VMEM((G, cols, C), F32))
        results = call(
            functools.partial(forward_kernel, dm, t, has_skip, has_mirror),
            [me], operands, outs, scratch,
            2 * dm.rows_of(k) * 28 * C * C,
        )
        pres.append(results[1])
        kept = results[2]
        current = hop(results[0], t, t + 1)
        if t == 0:
            marks = results[-1]
            raw, marks, _ = lax.optimization_barrier((kernel, marks, results[0]))
            targets = call(
                functools.partial(target_kernel, dm), [me, offsets], [marks],
                [shape(8, dm.rows_of(n - 1), F32)], [], 1000,
            )[0]
            kernel_t = call(
                functools.partial(flip_kernel, C), [], [raw],
                [shape(27 * C, C, BF)], [], 2 * 27 * C * C * 100,
            )[0]
        if has_mirror:
            later, current = lax.optimization_barrier((results[3], current))
            mirrors[n - 1 - t] = hop(later, t, n - 1 - t)

    t = n - 1
    skip = mirrors[t]
    branch = skip[t * G:t * G + size]
    for s in range(half + 1, n - 1):
        first = dm.fwd(s) * G
        branch = jnp.where(section == s, mirrors[s][first:first + size], branch)
    branch, _ = lax.optimization_barrier((branch, results[0]))
    branches = gather(branch, 0)
    outs = [
        shape(dm.rows_of(t - 1) + CARRY, C, BF),
        shape(size + CARRY, C, BF),
        shape(dm.rows_of(0), C, BF),
        shape(size, C, BF),
    ]
    results = call(
        functools.partial(last_kernel, dm),
        [me],
        [current, kernel, mixing, skip, kept, kernel_t, head, targets],
        outs,
        conv_scratch(dm, dm.rows_of(t + 1), dm.rows_of(t)) + [pltpu.VMEM((CARRY, C), F32)],
        4 * dm.rows_of(t) * 28 * C * C,
    )
    down = hop(results[0], t, t - 1)
    block, held = results[1], results[3]
    skip_grads = {0: hop(results[2], t, 0)}
    held = gather(held, 0)
    cells_all = micro * W * G

    for t in range(n - 2, -1, -1):
        has_skip = t < half - 1
        operands = [down, pres[t], block]
        if t > 0:
            operands += [kernel_t, mixing]
        if has_skip:
            operands.append(skip_grads[t])
        outs = [shape(size + CARRY, C, BF)]
        scratch = []
        if t > 0:
            outs.append(shape(dm.rows_of(t - 1) + CARRY, C, BF))
            if t > half:
                outs.append(shape(dm.rows_of(n - 1 - t), C, BF))
            scratch = conv_scratch(dm, dm.rows_of(t), dm.rows_of(t - 1))
        results = call(
            functools.partial(backward_kernel, dm, t, has_skip),
            [me], operands, outs, scratch,
            2 * dm.rows_of(max(t - 1, 0)) * 28 * C * C if t > 0 else 1000,
        )
        block = results[0]
        if t > 0:
            down = hop(results[1], t, t - 1)
            if t > half:
                skip_grads[n - 1 - t] = hop(results[2], t, n - 1 - t)

    held[0], _ = lax.optimization_barrier((held[0], block))
    xt, bt = call(
        functools.partial(turn_kernel, dm),
        [me], held + branches,
        [shape(9 * C, cells_all, BF), shape(C, cells_all, BF)],
        [pltpu.VMEM((cells_all + 2 * PAD, C), F32)],
        2 * 10 * cells_all * C * 100,
    )
    near = [block]
    for r in range(1, parts):
        near.append(rotate(block, r))
    *far, xt = lax.optimization_barrier((*near[1:], xt))
    near = [block] + far
    blocks = list(near)
    for e in range(1, micro):
        blocks += [swap(b, e) for b in near]
    operands = [xt, bt, *blocks]
    scratch = [
        pltpu.VMEM((micro * (W + 2) * G, C), BF),
        pltpu.VMEM((27, C, C), F32),
        pltpu.VMEM((slabs, 8, C), F32),
        pltpu.SemaphoreType.DMA((27,)),
    ]
    outs = [
        jax.ShapeDtypeStruct((9, 3, C, C), F32),
        shape(C, C, F32),
        shape(dm.offs, C, F32),
        shape(1, 1, F32),
    ]
    moved = nbytes(operands) + nbytes(outs)
    grad, mix, heads, loss = pl.pallas_call(
        functools.partial(weight_kernel, dm),
        name="weights",
        out_shape=outs,
        in_specs=[scalar()] + [whole()] * len(operands),
        out_specs=[pl.BlockSpec(memory_space=pl.ANY), whole(), whole(), whole()],
        scratch_shapes=scratch,
        compiler_params=pltpu.CompilerParams(
            vmem_limit_bytes=nbytes(operands) + nbytes(scratch[:3]) + SPARE
        ),
        cost_estimate=pl.CostEstimate(
            flops=2 * cells_all * 28 * C * C, bytes_accessed=moved, transcendentals=0
        ),
    )(me, *operands)
    return (
        loss[0, 0],
        grad.reshape((1, 3, 3, 3, C, C)),
        mix[None],
        jnp.transpose(heads),
    )


def solution(mesh):
    placed = (
        P(None, None, "slab", None, None),
        P(None, "slab", None, None),
        P(),
        P("section", None, None, None, None, None),
        P("section", None, None),
        P(),
    )
    return jax.shard_map(
        body,
        mesh=mesh,
        in_specs=placed,
        out_specs=(P(), P("section", None, None, None, None, None), P("section", None, None), P()),
        check_vma=False,
    )
```
